512 devices in a mesh: mach: 8 (over x, core), panel: 64 (over z, y).
Axes of the slice: x: 4, y: 8, z: 8, core: 2. Of those that a mesh axis runs over, the one named last changes fastest.
Arguments:
- adjoint: bfloat16 [8, 512, 4, 128], P('mach', 'panel'), may hold values from -6 to 6
- near_blocks: bfloat16 [8, 512, 8, 128, 128], P('mach', 'panel'), may hold values from -0.1875 to 0.1875
- pattern: int32 [512, 8], P('panel'), may hold values from 0 to 511, as said below
- trim_mask: int32 [8, 4], P('mach'), may hold values 0 or 1
- spline_blocks: bfloat16 [512, 6, 128, 128], P('panel'), may hold values from -0.21875 to 0.21875
- spline_owner: int32 [512, 6], P('panel'), may hold values from 0 to 63, all different within a row; in each aligned block of 8 rows (0 to 7, 8 to 15, ...) at most 2 rows name the same one
- spline_local: int32 [512, 6], P('panel'), may hold values from 0 to 7
- struct_inverse: bfloat16 [512, 128, 128], P('panel'), may hold values from -0.1875 to 0.1875
Outputs:
- panel_loads: float32 [8, 512, 4, 128], P('mach', 'panel')
- struct_adjoint: float32 [512, 4, 128], P('panel')
The draws below stay inside these ranges and needn't reach their ends.
Inputs may be any that keep to these rules, and one draw needn't show every extreme that they name: `pattern`: entry 0 of row i is i itself; entry 1 is the mirror block (i + 256) mod 512; every other entry lies within 8 blocks of its row, and each row has one entry exactly 8 blocks away unless that falls outside the grid, where it is clipped to the end. `spline_owner`: the targets of one row are different owners; among the rows of one device no owner is named more than 2 times, a bound that some block reaches.
All inputs are finite; a program needn't handle non-finite values. No bound on the sum of `trim_mask` on one device may be relied on, other than what follows from the above.
Results may differ from the reference program's by a relative error of at most 0.004.
Values may be sent and summed in bfloat16 or wider, within the bound.
A program may use at most 64 MiB of HBM per device.

```python
import math
import jax
import jax.numpy as jnp
import numpy as np
from jax import lax

BS = 128
NRHS = 4
NNZ = 8
S_PER = 6
NB_DEV = 8
SB_DEV = 8
MACHS = 8
OWNERS = 64
NPB = 512
NSB = 512
CAP = 2


def draw_pattern(key, part):
    first, second = jax.random.split(jax.random.fold_in(key, 17))
    blocks_all = jnp.arange(NPB, dtype=jnp.int32)
    columns = jnp.arange(NNZ, dtype=jnp.int32)
    offsets = jax.random.randint(first, (NPB, NNZ), -NB_DEV, NB_DEV + 1).astype(jnp.int32)
    signs = jax.random.randint(second, (NPB,), 0, 2).astype(jnp.int32) * 2 - 1
    far_column = 2 + blocks_all % (NNZ - 2)
    offsets = jnp.where(columns[None, :] == far_column[:, None], (signs * NB_DEV)[:, None], offsets)
    offsets = jnp.where(columns[None, :] == 0, 0, offsets)
    near = jnp.clip(blocks_all[:, None] + offsets, 0, NPB - 1).astype(jnp.int32)
    mirror = ((blocks_all + NPB // 2) % NPB).astype(jnp.int32)
    return jnp.where(columns[None, :] == 1, mirror[:, None], near).astype(jnp.int32)


def with_ends(drawn, rng, low, high):
    longest = drawn.shape.index(max(drawn.shape))
    spots = []
    for shift in (0, 1):
        where = [jax.random.randint(jax.random.fold_in(rng, axis), (), 0, length) for axis, length in enumerate(drawn.shape)]
        where[longest] = (where[longest] + shift) % drawn.shape[longest]
        spots.append(tuple(where))
    return drawn.at[spots[0]].set(low).at[spots[1]].set(high)


def block_scale(stream_key, dims, shards, least, largest):
    def one(position, blocks):
        heights = jax.random.uniform(jax.random.fold_in(jax.random.fold_in(stream_key, 6), position), (blocks,), jnp.float32, least / len(shards), largest / len(shards))
        return jnp.repeat(jnp.exp(heights), dims[position] // blocks).reshape((-1,) + (1,) * (len(dims) - position - 1))

    gain = one(*shards[0])
    for cut in shards[1:]:
        gain = gain * one(*cut)
    return gain


def shared_out(own_key, own, number, rows, number_of, top, reach, slope):
    ranking = jax.random.permutation(own_key, number_of)
    packed, usual = shares(number_of, rows * top, reach, slope, True), shares(number_of, rows * top, reach, slope, False)
    places = jnp.arange(number_of)

    def named(sizes, offset_by):
        used = int((sizes > 0).sum())
        fixed = max(1, used // 4)
        moved = fixed + (places - fixed + offset_by * (used - fixed)) % max(1, number_of - fixed)
        return jnp.zeros((number_of,), jnp.int32).at[ranking[jnp.where(places < fixed, places, moved)]].set(jnp.asarray(sizes, jnp.int32))

    sizes = jnp.where(number % 4 == 0, named(packed, number // 4), named(usual, number - number // 4 - 1))
    mixed = jax.random.permutation(jax.random.fold_in(own, 3), number_of)
    source_of, sink = mixed[0:number_of // 2 * 2:2], mixed[1:number_of // 2 * 2:2]
    slack = jnp.minimum(sizes[source_of] - 1, reach - sizes[sink]) // 2
    slack = jnp.where((source_of == ranking[0]) | (sink == ranking[0]) | (sizes[sink] == 0), 0, jnp.maximum(slack, 0))
    moved = jax.random.randint(jax.random.fold_in(own, 4), (number_of // 2,), 0, 1 << 20) % (slack + 1)
    sizes = sizes.at[source_of].add(-moved).at[sink].add(moved)
    items = jnp.searchsorted(jnp.cumsum(sizes), jnp.arange(rows * top), side="right").astype(jnp.int32)
    grid = items.reshape(top, rows).T
    grid = grid[jax.random.permutation(jax.random.fold_in(own, 1), rows)]
    offset_by = jax.random.randint(jax.random.fold_in(own, 2), (rows, 1), 0, top)
    return jnp.take_along_axis(grid, (jnp.arange(top)[None, :] + offset_by) % top, axis=1)


def shares(count, total, reach, skew, full):
    weights = [(1 << 20) // math.isqrt(standing ** skew) + 1 for standing in range(1, count + 1)]
    largest = reach if full else min(reach, max(-(-total // count), total * weights[0] // sum(weights)))
    least = 1 if total - largest >= count - 1 else 0
    holding, spare = [largest] + [least] * (count - 1), total - largest - least * (count - 1)
    while spare > 0:
        candidates = [i for i in range(1, count) if holding[i] < largest] or [i for i in range(1, count) if holding[i] < reach]
        mass, remaining = sum([weights[i] for i in candidates]), spare
        for i in candidates:
            addition = min(reach - holding[i], max(1, remaining * weights[i] // mass), spare)
            holding[i] = holding[i] + addition
            spare = spare - addition
    return np.array(holding)


def bell_draw(stream_key, extent, width, reach, shards=(), kind=jnp.bfloat16):
    entries = jax.random.normal(stream_key, extent, jnp.float32) * width
    if len(shards) > 0:
        entries = block_scale(stream_key, extent, shards, -0.22, 0.18) * entries
    return jnp.clip(entries, min=-reach, max=reach).astype(kind)


def setup_inputs(seed: int = 0) -> dict:
    key_of = jax.random.split(jax.random.key(seed), 9)
    adjoint = bell_draw(key_of[0], (MACHS, NPB, NRHS, BS), 1.0, 6.0, ((0, 8), (1, 64)))
    near_blocks = bell_draw(key_of[1], (MACHS, NPB, NNZ, BS, BS), (NNZ * BS) ** -0.5, 0.1875, ((0, 8), (1, 64)))
    pattern = draw_pattern(jax.random.fold_in(key_of[8], 71), 0)
    trim_mask = with_ends((jax.random.randint(key_of[3], (MACHS, NRHS), 0, 4) < 3).astype(jnp.int32), jax.random.fold_in(key_of[3], 1), 0, 1)
    spline_blocks = bell_draw(key_of[4], (NPB, S_PER, BS, BS), (BS * NB_DEV * S_PER // SB_DEV) ** -0.5, 0.21875, ((0, 64),))
    spline_owner_keys = jax.random.split(jax.random.fold_in(key_of[5], 1), NPB // NB_DEV)
    spline_owner_turns = jax.random.permutation(jax.random.fold_in(key_of[5], 3), NPB // NB_DEV)
    spline_owner = jax.vmap(lambda own, number: shared_out(jax.random.fold_in(key_of[5], 2), own, number, NB_DEV, OWNERS, S_PER, CAP, 2))(spline_owner_keys, spline_owner_turns).reshape((NPB, S_PER))
    spline_local = with_ends(jax.random.randint(key_of[6], (NPB, S_PER), 0, SB_DEV), jax.random.fold_in(key_of[6], 1), 0, SB_DEV - 1).astype(jnp.int32)
    struct_inverse = bell_draw(key_of[7], (NSB, BS, BS), (BS * MACHS) ** -0.5, 0.1875, ((0, 64),))
    return {"adjoint": adjoint, "near_blocks": near_blocks, "pattern": pattern, "trim_mask": trim_mask, "spline_blocks": spline_blocks, "spline_owner": spline_owner, "spline_local": spline_local, "struct_inverse": struct_inverse}


def reference(adjoint, near_blocks, pattern, trim_mask, spline_blocks, spline_owner, spline_local, struct_inverse):
    targets = (spline_owner * SB_DEV + spline_local).reshape(-1).astype(jnp.int32)
    spline_wide = spline_blocks.astype(jnp.float32)

    def one_mach(which):
        pressures = adjoint[which]
        picked = pressures[pattern].astype(jnp.float32)
        blocks = near_blocks[which].astype(jnp.float32)
        near = jnp.einsum('bkrp,bkpq->brq', picked, blocks)
        gate = trim_mask[which].astype(jnp.float32)
        loads = near * gate[None, :, None]
        rounded = lax.optimization_barrier(loads.astype(jnp.bfloat16)).astype(jnp.float32)
        contrib = jnp.einsum('brp,bspq->bsrq', rounded, spline_wide)
        summed = jax.ops.segment_sum(contrib.reshape(-1, NRHS, BS), targets, NSB)
        return loads, summed

    panel_loads, per_mach = lax.map(one_mach, jnp.arange(MACHS, dtype=jnp.int32))
    struct_loads = jnp.sum(per_mach, axis=0)
    struct_rounded = lax.optimization_barrier(struct_loads.astype(jnp.bfloat16)).astype(jnp.float32)
    struct_adjoint = jnp.einsum('trp,tpq->trq', struct_rounded, struct_inverse.astype(jnp.float32))
    return panel_loads, struct_adjoint
```

```python
import jax
import jax.numpy as jnp
from jax import lax
from jax.experimental import pallas as pl
from jax.experimental.pallas import tpu as pltpu
from jax.sharding import PartitionSpec as P

MESH = pl.DeviceIdType.MESH
F32 = jnp.float32
BF16 = jnp.bfloat16
MACHS = 8
PANELS = 64
RING = 8
ROWS = 8
NNZ = 8
TARGETS = 6
RHS = 4
CAP = 2
LANES = TARGETS * ROWS * RHS
SLOTS = PANELS * CAP * RHS


def iota(shape, axis):
    return lax.broadcasted_iota(jnp.int32, shape, axis)


def ones_where(cond):
    return jnp.where(cond, 1.0, 0.0).astype(BF16)


def kernel(
    adj_ref,
    near_hbm,
    pat_ref,
    mask_ref,
    spline_hbm,
    own_ref,
    loc_ref,
    inv_hbm,
    loads_ref,
    struct_ref,
    near_ref,
    spline_ref,
    inv_ref,
    pool,
    mirror,
    near_acc,
    mach_buf,
    place,
    pick,
    tab,
    ytab,
    ycomp,
    ztab,
    send_buf,
    recv_buf,
    load_sem,
    halo_send,
    halo_recv,
    ring_send,
    ring_recv,
    mach_send,
    mach_recv,
    all_send,
    all_recv,
):
    m = lax.axis_index("mach")
    p = lax.axis_index("panel")
    z = p // RING
    y = p % RING

    loads = [
        pltpu.make_async_copy(near_hbm, near_ref, load_sem.at[0]),
        pltpu.make_async_copy(spline_hbm, spline_ref, load_sem.at[1]),
        pltpu.make_async_copy(inv_hbm, inv_ref, load_sem.at[2]),
    ]
    barrier = pltpu.get_barrier_semaphore()

    def row_peer(j):
        return (m, z * RING + (y + j) % RING)

    def column_peer(j):
        return (m, ((z + j) % RING) * RING + y)

    def mach_peer(j):
        return ((m + j) % MACHS, p)

    right = (m, (p + 1) % PANELS)
    left = (m, (p + PANELS - 1) % PANELS)
    opposite = (m, (p + PANELS // 2) % PANELS)

    peers = [left, right]
    for j in range(1, RING):
        peers += [row_peer(j), column_peer(j), mach_peer(j)]
    for peer in peers:
        pl.semaphore_signal(barrier, inc=1, device_id=peer, device_id_type=MESH)
    for copy in loads:
        copy.start()

    own = own_ref[...].astype(F32)
    loc = loc_ref[...].astype(F32)
    lane = iota((ROWS, LANES), 1)
    sub = iota((ROWS, LANES), 0)
    lane_s = lane // (ROWS * RHS)
    lane_i = (lane // RHS) % ROWS
    own_rows = jnp.zeros((ROWS, LANES), F32)
    loc_rows = jnp.zeros((ROWS, LANES), F32)
    for s in range(TARGETS):
        own_rows = jnp.where(lane_s == s, own[:, s : s + 1], own_rows)
        loc_rows = jnp.where(lane_s == s, loc[:, s : s + 1], loc_rows)
    mine = sub == lane_i
    own_lane = jnp.sum(jnp.where(mine, own_rows, 0.0), axis=0, keepdims=True)
    loc_lane = jnp.sum(jnp.where(mine, loc_rows, 0.0), axis=0, keepdims=True)
    same = jnp.zeros((ROWS, LANES), F32)
    for s in range(TARGETS):
        same = same + jnp.where(own[:, s : s + 1] == own_lane, 1.0, 0.0)
    slot = jnp.sum(jnp.where(sub < lane_i, same, 0.0), axis=0, keepdims=True)
    dest = own_lane * CAP + slot
    lane_r = (iota((1, LANES), 1) % RHS).astype(F32)
    place[...] = ones_where(iota((SLOTS, LANES), 0).astype(F32) == dest * RHS + lane_r)
    chosen = ones_where(iota((PANELS * CAP, LANES), 0).astype(F32) == dest)
    weights = jnp.broadcast_to(
        jnp.where(lane_r == 0.0, loc_lane + 1.0, 0.0), (ROWS, LANES)
    ).astype(BF16)
    tab[...] = lax.dot_general(
        weights, chosen, (((1,), (1,)), ((), ())), preferred_element_type=F32
    )
    pool[ROWS : 2 * ROWS] = adj_ref[...]

    pl.semaphore_wait(barrier, len(peers))

    def send(src, dst, send_sem, recv_sem, peer):
        copy = pltpu.make_async_remote_copy(
            src_ref=src,
            dst_ref=dst,
            send_sem=send_sem,
            recv_sem=recv_sem,
            device_id=peer,
            device_id_type=MESH,
        )
        copy.start()
        return copy

    def drain(ref, sem):
        pltpu.make_async_copy(ref, ref, sem).wait()

    halos = [
        send(adj_ref, mirror, halo_send.at[0], halo_recv.at[0], opposite),
        send(adj_ref, pool.at[pl.ds(0, ROWS)], halo_send.at[1], halo_recv.at[1], right),
        send(adj_ref, pool.at[pl.ds(2 * ROWS, ROWS)], halo_send.at[2], halo_recv.at[2], left),
    ]
    for j in range(1, RING):
        send(tab, ytab.at[y], ring_send.at[0], ring_recv.at[0], row_peer(j))
    ytab[y] = tab[...]

    loads[0].wait()
    halos[1].wait_recv()
    halos[2].wait_recv()
    for i in range(ROWS):
        picked = [
            pool[jnp.clip(pat_ref[i, k] - p * ROWS + ROWS, 0, 3 * ROWS - 1)]
            for k in range(2, NNZ)
        ]
        near_acc[RHS * i : RHS * (i + 1), :] = jnp.dot(
            pool[ROWS + i], near_ref[i, 0], preferred_element_type=F32
        ) + jnp.dot(
            jnp.concatenate(picked, axis=1),
            near_ref[i, 2:NNZ].reshape((NNZ - 2) * 128, 128),
            preferred_element_type=F32,
        )

    drain(ytab.at[pl.ds(0, RING - 1)], ring_recv.at[0])
    sub8 = iota((RING, 128), 0)
    comp = jnp.zeros((RING, 128), F32)
    for j in range(RING):
        comp = jnp.where(sub8 == j, ytab[j], comp)
    ycomp[...] = comp
    for j in range(1, RING):
        send(ycomp, ztab.at[z], ring_send.at[1], ring_recv.at[1], column_peer(j))
    ztab[z] = ycomp[...]

    row32 = iota((ROWS * RHS, 1), 0)
    gate = jnp.zeros((ROWS * RHS, 1), F32)
    for r in range(RHS):
        gate = jnp.where(row32 % RHS == r, mask_ref[0, r].astype(F32), gate)

    halos[0].wait_recv()
    for i in range(ROWS):
        near_acc[RHS * i : RHS * (i + 1), :] += jnp.dot(
            mirror[i], near_ref[i, 1], preferred_element_type=F32
        )
    masked = near_acc[...] * gate
    loads_ref[...] = masked
    mach_buf[m] = masked.astype(BF16)
    for j in range(1, MACHS):
        send(mach_buf.at[m], mach_buf.at[m], mach_send, mach_recv, mach_peer(j))

    drain(ztab.at[pl.ds(0, RING - 1)], ring_recv.at[1])
    lane5 = iota((128, SLOTS), 1)
    wanted = ones_where(iota((128, SLOTS), 0) == p * CAP + (lane5 // RHS) % CAP)
    blocks = jnp.dot(
        ztab[...].reshape(PANELS, 128).astype(BF16), wanted, preferred_element_type=F32
    )
    from_panel = iota((PANELS, SLOTS), 0) == iota((PANELS, SLOTS), 1) // (CAP * RHS)
    block_lane = jnp.sum(jnp.where(from_panel, blocks, 0.0), axis=0, keepdims=True)
    row5 = iota((ROWS * RHS, SLOTS), 0)
    col5 = iota((ROWS * RHS, SLOTS), 1)
    pick[...] = ones_where(
        (block_lane == (row5 // RHS + 1).astype(F32)) & (col5 % RHS == row5 % RHS)
    )

    loads[1].wait()
    drain(mach_buf.at[pl.ds(0, MACHS - 1)], mach_recv)
    total = mach_buf[0].astype(F32)
    for j in range(1, MACHS):
        total = total + mach_buf[j].astype(F32)
    high = total.astype(BF16).astype(F32)
    both = jnp.concatenate([high, total - high], axis=0)
    row64 = (iota((2 * ROWS * RHS, 128), 0) // RHS) % ROWS
    spread = jnp.concatenate(
        [jnp.where(row64 == i, both, 0.0).astype(BF16) for i in range(ROWS)], axis=1
    )
    contrib = []
    for s in range(TARGETS):
        out = jnp.dot(
            spread,
            spline_ref[:, s].reshape(ROWS * 128, 128),
            preferred_element_type=F32,
        )
        contrib.append((out[: ROWS * RHS] + out[ROWS * RHS :]).astype(BF16))
    packed = jnp.dot(
        place[...], jnp.concatenate(contrib, axis=0), preferred_element_type=F32
    )
    send_buf[...] = packed.astype(BF16).reshape(PANELS, CAP * RHS, 128)

    def post(j, carry):
        peer = (p + PANELS // 2 + j) % PANELS

        @pl.when(peer != p)
        def _():
            send(send_buf.at[peer], recv_buf.at[p], all_send, all_recv, (m, peer))

        return carry

    lax.fori_loop(0, PANELS, post, 0)
    recv_buf[p] = send_buf[p]

    loads[2].wait()
    drain(recv_buf.at[pl.ds(0, PANELS - 1)], all_recv)
    found = jnp.dot(
        pick[...],
        recv_buf[...].reshape(SLOTS, 128),
        preferred_element_type=F32,
    )
    row_block = iota((ROWS * RHS, 128), 0) // RHS
    spread = jnp.concatenate(
        [jnp.where(row_block == t, found, 0.0).astype(BF16) for t in range(ROWS)], axis=1
    )
    struct_ref[...] = jnp.dot(
        spread, inv_ref[...].reshape(ROWS * 128, 128), preferred_element_type=F32
    )

    for copy in halos:
        copy.wait_send()
    for stage, ref in enumerate((ytab, ztab)):
        drain(ref.at[pl.ds(0, RING - 1)], ring_send.at[stage])
    drain(mach_buf.at[pl.ds(0, MACHS - 1)], mach_send)
    drain(send_buf.at[pl.ds(0, PANELS - 1)], all_send)


def on_device(adjoint, near, pattern, mask, spline, owner, local, inverse):
    vmem = pl.BlockSpec(memory_space=pltpu.VMEM)
    smem = pl.BlockSpec(memory_space=pltpu.SMEM)
    hbm = pl.BlockSpec(memory_space=pl.ANY)
    rows = ROWS * RHS
    dma = pltpu.SemaphoreType.DMA
    loads, struct = pl.pallas_call(
        kernel,
        out_shape=(
            jax.ShapeDtypeStruct((rows, 128), F32),
            jax.ShapeDtypeStruct((rows, 128), F32),
        ),
        in_specs=[vmem, hbm, smem, smem, hbm, vmem, vmem, hbm],
        out_specs=(vmem, vmem),
        scratch_shapes=[
            pltpu.VMEM((ROWS, NNZ, 128, 128), BF16),
            pltpu.VMEM((ROWS, TARGETS, 128, 128), BF16),
            pltpu.VMEM((ROWS, 128, 128), BF16),
            pltpu.VMEM((3 * ROWS, RHS, 128), BF16),
            pltpu.VMEM((ROWS, RHS, 128), BF16),
            pltpu.VMEM((rows, 128), F32),
            pltpu.VMEM((MACHS, rows, 128), BF16),
            pltpu.VMEM((SLOTS, LANES), BF16),
            pltpu.VMEM((rows, SLOTS), BF16),
            pltpu.VMEM((RING, 128), F32),
            pltpu.VMEM((RING, RING, 128), F32),
            pltpu.VMEM((RING, 128), F32),
            pltpu.VMEM((RING, RING, 128), F32),
            pltpu.VMEM((PANELS, CAP * RHS, 128), BF16),
            pltpu.VMEM((PANELS, CAP * RHS, 128), BF16),
            dma((3,)),
            dma((3,)),
            dma((3,)),
            dma((2,)),
            dma((2,)),
            dma,
            dma,
            dma,
            dma,
        ],
        compiler_params=pltpu.CompilerParams(collective_id=0, has_side_effects=True),
        name="load_transfer",
    )(adjoint[0], near[0], pattern, mask, spline, owner, local, inverse)
    return loads.reshape(1, ROWS, RHS, 128), struct.reshape(ROWS, RHS, 128)


def solution(mesh):
    in_specs = (
        P("mach", "panel", None, None),
        P("mach", "panel", None, None, None),
        P("panel", None),
        P("mach", None),
        P("panel", None, None, None),
        P("panel", None),
        P("panel", None),
        P("panel", None, None),
    )
    out_specs = (P("mach", "panel", None, None), P("panel", None, None))
    return jax.shard_map(
        on_device, mesh=mesh, in_specs=in_specs, out_specs=out_specs, check_vma=False
    )
```

```python
import jax
import jax.numpy as jnp
from jax import lax
from jax.experimental import pallas as pl
from jax.experimental.pallas import tpu as pltpu
from jax.sharding import PartitionSpec as P

MESH = pl.DeviceIdType.MESH
F32 = jnp.float32
BF16 = jnp.bfloat16
MACHS = 8
PANELS = 64
RING = 8
ROWS = 8
NNZ = 8
TARGETS = 6
RHS = 4
CAP = 2
LANES = TARGETS * ROWS * RHS
SERVED = PANELS // 2
SLOTS = SERVED * CAP * RHS


def iota(shape, axis):
    return lax.broadcasted_iota(jnp.int32, shape, axis)


def ones_where(cond):
    return jnp.where(cond, 1.0, 0.0).astype(BF16)


def kernel(
    adj_hbm,
    near_hbm,
    pat_hbm,
    mask_hbm,
    spline_hbm,
    own_hbm,
    loc_hbm,
    inv_hbm,
    loads_ref,
    struct_ref,
    near_ref,
    spline_ref,
    inv_ref,
    own_ref,
    loc_ref,
    pat_ref,
    mask_ref,
    pool,
    mirror,
    relay,
    near_acc,
    mach_buf,
    place,
    pick,
    tab,
    ytab,
    ycomp,
    ztab,
    send_buf,
    recv_buf,
    load_sem,
    halo_send,
    halo_recv,
    relay_send,
    relay_recv,
    pass_send,
    ring_send,
    ring_recv,
    mach_send,
    mach_recv,
    all_send,
    all_recv,
    core_send,
    core_recv,
    next_ready,
    wrap_ready,
    row_near,
    row_far,
    col_ready,
    mach_ready,
    mach_near,
    mach_far,
    row_in,
):
    m = lax.axis_index("mach")
    p = lax.axis_index("panel")
    z = p // RING
    y = p % RING
    core = m % 2
    barrier = pltpu.get_barrier_semaphore()

    def signal(sem, peer):
        pl.semaphore_signal(sem, inc=1, device_id=peer, device_id_type=MESH)

    def row_peer(j):
        return (m, z * RING + (y + j) % RING)

    def column_peer(j):
        return (m, ((z + j) % RING) * RING + y)

    def mach_peer(j):
        return ((m + j) % MACHS, p)

    half = RING // 2
    x = m // 2
    chips = MACHS // 2
    x_up = ((m + 2) % MACHS, p)
    x_down = ((m + MACHS - 2) % MACHS, p)
    other = (m + 1 - 2 * core, p)
    ends_row = (y == RING - 1) & (z < RING - 1)
    opens_row = (y == 0) & (z > 0)
    row_right = (m, z * RING + (y + 1) % RING)
    row_left = (m, z * RING + (y + RING - 1) % RING)

    @pl.when(x < chips - 1)
    def _():
        signal(barrier, x_up)

    @pl.when(x == 0)
    def _():
        signal(barrier, x_down)

    @pl.when(core == 1)
    def _():
        signal(barrier, other)

    @pl.when(y < half)
    def _():
        signal(barrier, row_right)

    @pl.when((y == 0) | (y > half))
    def _():
        signal(barrier, row_left)

    @pl.when(ends_row)
    def _():
        signal(barrier, (m, p + 1))

    def each(low, high, act):
        def step(k, carry):
            act(k)
            return carry

        lax.fori_loop(low, high, step, 0)

    each(z + 1, RING, lambda k: signal(barrier, (m, k * RING + y)))

    pairs = [
        (adj_hbm, pool.at[pl.ds(ROWS, ROWS)]),
        (own_hbm, own_ref),
        (loc_hbm, loc_ref),
        (pat_hbm, pat_ref),
        (mask_hbm, mask_ref),
        (near_hbm, near_ref),
        (spline_hbm, spline_ref),
        (inv_hbm, inv_ref),
    ]
    loads = [
        pltpu.make_async_copy(src, dst, load_sem.at[n]) for n, (src, dst) in enumerate(pairs)
    ]
    adj_load, own_load, loc_load, pat_load, mask_load, near_load, spline_load, inv_load = loads
    for copy in loads:
        copy.start()

    def send(src, dst, send_sem, recv_sem, peer):
        copy = pltpu.make_async_remote_copy(
            src_ref=src,
            dst_ref=dst,
            send_sem=send_sem,
            recv_sem=recv_sem,
            device_id=peer,
            device_id_type=MESH,
        )
        copy.start()
        return copy

    def drain(ref, sem):
        pltpu.make_async_copy(ref, ref, sem).wait()

    row_count = jnp.where(y == 0, opens_row.astype(jnp.int32), jnp.where(y == half, 2, 1))
    mach_count = jnp.where(x == 0, 0, jnp.where(x == chips - 1, 2, 1)) + 1 - core
    count = z + mach_count + row_count

    @pl.when(count > 0)
    def _():
        pl.semaphore_wait(barrier, count)

    adj = pool.at[pl.ds(ROWS, ROWS)]
    after_left = opens_row | ((y > 0) & (y <= half))
    after_right = (y >= half) & (y < RING - 1)
    before_left = y > half
    before_right = (y < half) | ends_row

    @pl.when(z >= RING - 2)
    def _():
        signal(col_ready.at[z], (m, y))

    @pl.when((z == half) | (z == half + 1))
    def _():
        signal(col_ready.at[z], (m, (half - 1) * RING + y))

    @pl.when(after_left)
    def _():
        signal(next_ready.at[1], (m, p - 1))

    @pl.when(after_right)
    def _():
        signal(next_ready.at[0], (m, p + 1))

    @pl.when(z == half - 1)
    def _():
        signal(col_ready.at[z], (m, y))
        signal(col_ready.at[z], (m, RING + y))

    adj_load.wait()

    @pl.when(z >= half)
    def _():
        send(adj, mirror, halo_send.at[0], halo_recv.at[0], (m, p - half * RING))

    def to_left():
        send(adj, pool.at[pl.ds(2 * ROWS, ROWS)], halo_send.at[2], halo_recv.at[2], (m, p - 1))

    def to_right():
        send(adj, pool.at[pl.ds(0, ROWS)], halo_send.at[1], halo_recv.at[1], (m, p + 1))

    pl.when(after_left)(to_left)
    pl.when(after_right)(to_right)

    @pl.when(y == RING - 1)
    def _():
        signal(wrap_ready, row_right)

    @pl.when(core == 0)
    def _():
        signal(mach_ready, other)

    @pl.when(x > 0)
    def _():
        signal(mach_ready, x_down)

    @pl.when(x == chips - 1)
    def _():
        signal(mach_ready, x_up)

    def answer(k):
        told = (
            (z >= RING - 2) & (k == 0)
            | ((z == half) | (z == half + 1)) & (k == half - 1)
            | (z == half - 1) & (k < 2)
        )

        @pl.when(jnp.logical_not(told))
        def _():
            signal(col_ready.at[z], (m, k * RING + y))

    each(0, z, answer)

    @pl.when((z >= 2) & (z < half))
    def _():
        send(adj, relay.at[z - 2], halo_send.at[0], relay_recv.at[z - 2], (m, p - z * RING))

    @pl.when(before_left)
    def _():
        pl.semaphore_wait(next_ready.at[0], 1)
        to_left()

    @pl.when(before_right)
    def _():
        pl.semaphore_wait(next_ready.at[1], 1)
        to_right()

    @pl.when(z < 2)
    def _():
        pl.semaphore_wait(col_ready.at[half - 1], 1)
        send(
            adj, relay.at[z], halo_send.at[0], relay_recv.at[z], (m, p + (half - 1 - z) * RING)
        )

    @pl.when(y == 0)
    def _():
        pl.semaphore_wait(wrap_ready, 1)

    @pl.when(mach_count < 3)
    def _():
        pl.semaphore_wait(mach_ready, 3 - mach_count)

    signal(mach_near, x_up)
    signal(mach_near, x_down)
    signal(mach_near, other)
    signal(row_near, row_right)
    signal(row_near, row_left)

    own_load.wait()
    loc_load.wait()
    own = own_ref[...].astype(F32)
    loc = loc_ref[...].astype(F32)
    lane = iota((ROWS, LANES), 1)
    sub = iota((ROWS, LANES), 0)
    lane_s = lane // (ROWS * RHS)
    lane_i = (lane // RHS) % ROWS
    own_rows = jnp.zeros((ROWS, LANES), F32)
    loc_rows = jnp.zeros((ROWS, LANES), F32)
    for s in range(TARGETS):
        own_rows = jnp.where(lane_s == s, own[:, s : s + 1], own_rows)
        loc_rows = jnp.where(lane_s == s, loc[:, s : s + 1], loc_rows)
    mine = sub == lane_i
    own_lane = jnp.sum(jnp.where(mine, own_rows, 0.0), axis=0, keepdims=True)
    loc_lane = jnp.sum(jnp.where(mine, loc_rows, 0.0), axis=0, keepdims=True)
    same = jnp.zeros((ROWS, LANES), F32)
    for s in range(TARGETS):
        same = same + jnp.where(own[:, s : s + 1] == own_lane, 1.0, 0.0)
    slot = jnp.sum(jnp.where(sub < lane_i, same, 0.0), axis=0, keepdims=True)
    dest = own_lane * CAP + slot
    lane_r = (iota((1, LANES), 1) % RHS).astype(F32)
    chosen = ones_where(iota((PANELS * CAP, LANES), 0).astype(F32) == dest)
    weights = jnp.broadcast_to(
        jnp.where(lane_r == 0.0, loc_lane + 1.0, 0.0), (ROWS, LANES)
    ).astype(BF16)
    tab[...] = lax.dot_general(
        weights, chosen, (((1,), (1,)), ((), ())), preferred_element_type=F32
    )

    owner_row = iota((SLOTS, LANES), 0)
    owner_row = (owner_row // (CAP * RHS)) * (2 * CAP * RHS) + owner_row % (CAP * RHS)
    owner_row = owner_row + core * (CAP * RHS)
    place[...] = ones_where(owner_row.astype(F32) == dest * RHS + lane_r)

    def pass_on(slot, child):
        pltpu.make_async_copy(relay.at[slot], relay.at[slot], relay_recv.at[slot]).wait()
        pl.semaphore_wait(col_ready.at[child], 1)
        send(
            relay.at[slot], mirror, pass_send.at[slot], halo_recv.at[0], (m, child * RING + y)
        )

    @pl.when(z == 3)
    def _():
        pass_on(0, 4)
        pass_on(1, 5)

    @pl.when(z == 0)
    def _():
        pass_on(0, 6)
        pass_on(1, 7)

    pl.semaphore_wait(mach_near, 3)
    signal(mach_far, other)
    pl.semaphore_wait(row_near, 2)
    for j in (1, 2, RING - 2, RING - 1):
        signal(row_far, row_peer(j))

    pat_load.wait()
    near_load.wait()

    @pl.when(p > 0)
    def _():
        drain(mirror, halo_recv.at[1])

    @pl.when(p < PANELS - 1)
    def _():
        drain(mirror, halo_recv.at[2])

    for i in range(ROWS):
        picked = [
            pool[jnp.clip(pat_ref[i, k] - p * ROWS + ROWS, 0, 3 * ROWS - 1)]
            for k in range(2, NNZ)
        ]
        near_acc[RHS * i : RHS * (i + 1), :] = jnp.dot(
            pool[ROWS + i], near_ref[i, 0], preferred_element_type=F32
        ) + jnp.dot(
            jnp.concatenate(picked, axis=1),
            near_ref[i, 2:NNZ].reshape((NNZ - 2) * 128, 128),
            preferred_element_type=F32,
        )

    mask_load.wait()
    row32 = iota((ROWS * RHS, 1), 0)
    gate = jnp.zeros((ROWS * RHS, 1), F32)
    for r in range(RHS):
        gate = jnp.where(row32 % RHS == r, mask_ref[0, r].astype(F32), gate)

    pl.semaphore_wait(row_far, 4)
    for j in range(1, RING):
        send(tab, ytab.at[y], ring_send.at[0], ring_recv.at[0], row_peer(j))
    ytab[y] = tab[...]

    for k in range(1, RING):
        early = (z == 0) & (k in (3, 6, 7)) | (z == 1) & (k == 3) | (z == 3) & (k in (4, 5))

        @pl.when((k > z) & jnp.logical_not(early))
        def _():
            pl.semaphore_wait(col_ready.at[k], 1)

    for j in range(1, RING):
        signal(row_in, column_peer(j))

    pl.semaphore_wait(mach_far, 1)
    drain(mirror, halo_recv.at[0])
    for i in range(ROWS):
        near_acc[RHS * i : RHS * (i + 1), :] += jnp.dot(
            mirror[i], near_ref[i, 1], preferred_element_type=F32
        )
    masked = near_acc[...] * gate
    mach_buf[m] = masked.astype(BF16)
    for j in (4, 3, 5, 2, 6, 1, 7):
        send(mach_buf.at[m], mach_buf.at[m], mach_send, mach_recv, mach_peer(j))
    loads_ref[...] = masked

    spline_load.wait()
    drain(mach_buf.at[pl.ds(0, MACHS - 1)], mach_recv)
    total = mach_buf[0].astype(F32)
    for j in range(1, MACHS):
        total = total + mach_buf[j].astype(F32)
    high = total.astype(BF16).astype(F32)
    both = jnp.concatenate([high, total - high], axis=0)
    row64 = (iota((2 * ROWS * RHS, 128), 0) // RHS) % ROWS
    spread = jnp.concatenate(
        [jnp.where(row64 == i, both, 0.0).astype(BF16) for i in range(ROWS)], axis=1
    )
    contrib = []
    for s in range(TARGETS):
        out = jnp.dot(
            spread,
            spline_ref[:, s].reshape(ROWS * 128, 128),
            preferred_element_type=F32,
        )
        contrib.append((out[: ROWS * RHS] + out[ROWS * RHS :]).astype(BF16))
    packed = jnp.dot(
        place[...], jnp.concatenate(contrib, axis=0), preferred_element_type=F32
    )
    send_buf[...] = packed.astype(BF16).reshape(SERVED, CAP * RHS, 128)

    serves = y % 2 == core
    pl.semaphore_wait(row_in, RING - 1)

    def post(j, carry):
        far = j // (RING // 2)
        side = 1 - 2 * (far % 2)
        to_z = (z + RING // 2 + side * ((far + 1) // 2) + RING) % RING
        to_y = ((y // 2 + 2 + j % (RING // 2)) % (RING // 2)) * 2 + core
        peer = to_z * RING + to_y

        @pl.when(peer != p)
        def _():
            send(send_buf.at[peer // 2], recv_buf.at[p], all_send, all_recv, (m, peer))

        return carry

    lax.fori_loop(0, SERVED, post, 0)

    drain(ytab.at[pl.ds(0, RING - 1)], ring_recv.at[0])
    sub8 = iota((RING, 128), 0)
    comp = jnp.zeros((RING, 128), F32)
    for j in range(RING):
        comp = jnp.where(sub8 == j, ytab[j], comp)
    ycomp[...] = comp
    for j in range(1, RING):
        send(ycomp, ztab.at[z], ring_send.at[1], ring_recv.at[1], column_peer(j))
    ztab[z] = ycomp[...]

    drain(ztab.at[pl.ds(0, RING - 1)], ring_recv.at[1])
    inv_load.wait()

    @pl.when(serves)
    def _():
        recv_buf[p] = send_buf[p // 2]
        lane5 = iota((128, PANELS * CAP * RHS), 1)
        wanted = ones_where(iota((128, PANELS * CAP * RHS), 0) == p * CAP + (lane5 // RHS) % CAP)
        blocks = jnp.dot(
            ztab[...].reshape(PANELS, 128).astype(BF16), wanted, preferred_element_type=F32
        )
        shape = (PANELS, PANELS * CAP * RHS)
        from_panel = iota(shape, 0) == iota(shape, 1) // (CAP * RHS)
        block_lane = jnp.sum(jnp.where(from_panel, blocks, 0.0), axis=0, keepdims=True)
        shape = (ROWS * RHS, PANELS * CAP * RHS)
        row5 = iota(shape, 0)
        col5 = iota(shape, 1)
        pick[...] = ones_where(
            (block_lane == (row5 // RHS + 1).astype(F32)) & (col5 % RHS == row5 % RHS)
        )
        drain(recv_buf.at[pl.ds(0, PANELS - 1)], all_recv)
        found = jnp.dot(
            pick[...],
            recv_buf[...].reshape(PANELS * CAP * RHS, 128),
            preferred_element_type=F32,
        )
        row_block = iota((ROWS * RHS, 128), 0) // RHS
        wide = jnp.concatenate(
            [jnp.where(row_block == t, found, 0.0).astype(BF16) for t in range(ROWS)], axis=1
        )
        struct_ref[...] = jnp.dot(
            wide, inv_ref[...].reshape(ROWS * 128, 128), preferred_element_type=F32
        )
        send(struct_ref, struct_ref, core_send, core_recv, other)
        drain(send_buf.at[pl.ds(0, SERVED - 1)], all_send)
        drain(struct_ref, core_send)

    @pl.when(jnp.logical_not(serves))
    def _():
        drain(send_buf, all_send)
        drain(struct_ref, core_recv)

    drain(mirror, halo_send.at[0])

    @pl.when(p < PANELS - 1)
    def _():
        drain(mirror, halo_send.at[1])

    @pl.when(p > 0)
    def _():
        drain(mirror, halo_send.at[2])

    @pl.when((z == 0) | (z == 3))
    def _():
        drain(mirror, pass_send.at[0])
        drain(mirror, pass_send.at[1])

    for stage, ref in enumerate((ytab, ztab)):
        drain(ref.at[pl.ds(0, RING - 1)], ring_send.at[stage])
    drain(mach_buf.at[pl.ds(0, MACHS - 1)], mach_send)


def hand_on(loads_ref, struct_ref, loads_out, struct_out):
    loads_out[...] = loads_ref[...]
    struct_out[...] = struct_ref[...]


def on_device(adjoint, near, pattern, mask, spline, owner, local, inverse):
    vmem = pl.BlockSpec(memory_space=pltpu.VMEM)
    hbm = pl.BlockSpec(memory_space=pl.ANY)
    rows = ROWS * RHS
    dma = pltpu.SemaphoreType.DMA
    regular = pltpu.SemaphoreType.REGULAR
    loads, struct = pl.pallas_call(
        kernel,
        out_shape=(
            jax.ShapeDtypeStruct((rows, 128), F32),
            jax.ShapeDtypeStruct((rows, 128), F32),
        ),
        in_specs=[hbm] * 8,
        out_specs=(vmem, vmem),
        scratch_shapes=[
            pltpu.VMEM((ROWS, NNZ, 128, 128), BF16),
            pltpu.VMEM((ROWS, TARGETS, 128, 128), BF16),
            pltpu.VMEM((ROWS, 128, 128), BF16),
            pltpu.VMEM((ROWS, TARGETS), jnp.int32),
            pltpu.VMEM((ROWS, TARGETS), jnp.int32),
            pltpu.SMEM((ROWS, NNZ), jnp.int32),
            pltpu.SMEM((1, RHS), jnp.int32),
            pltpu.VMEM((3 * ROWS, RHS, 128), BF16),
            pltpu.VMEM((ROWS, RHS, 128), BF16),
            pltpu.VMEM((2, ROWS, RHS, 128), BF16),
            pltpu.VMEM((rows, 128), F32),
            pltpu.VMEM((MACHS, rows, 128), BF16),
            pltpu.VMEM((SLOTS, LANES), BF16),
            pltpu.VMEM((rows, PANELS * CAP * RHS), BF16),
            pltpu.VMEM((RING, 128), F32),
            pltpu.VMEM((RING, RING, 128), F32),
            pltpu.VMEM((RING, 128), F32),
            pltpu.VMEM((RING, RING, 128), F32),
            pltpu.VMEM((SERVED, CAP * RHS, 128), BF16),
            pltpu.VMEM((PANELS, CAP * RHS, 128), BF16),
            dma((8,)),
            dma((3,)),
            dma((3,)),
            dma((2,)),
            dma((2,)),
            dma((2,)),
            dma((2,)),
            dma((2,)),
            dma,
            dma,
            dma,
            dma,
            dma,
            dma,
            regular((2,)),
            regular,
            regular,
            regular,
            regular((RING,)),
            regular,
            regular,
            regular,
            regular,
        ],
        compiler_params=pltpu.CompilerParams(collective_id=0, has_side_effects=True),
        name="load_transfer",
    )(adjoint[0], near[0], pattern, mask, spline, owner, local, inverse)
    out = jax.ShapeDtypeStruct((rows, 128), F32)
    loads, struct = pl.pallas_call(
        hand_on,
        out_shape=(out, out),
        in_specs=[vmem, vmem],
        out_specs=(vmem, vmem),
        name="hand_on",
    )(loads, struct)
    return loads.reshape(1, ROWS, RHS, 128), struct.reshape(ROWS, RHS, 128)


def solution(mesh):
    in_specs = (
        P("mach", "panel", None, None),
        P("mach", "panel", None, None, None),
        P("panel", None),
        P("mach", None),
        P("panel", None, None, None),
        P("panel", None),
        P("panel", None),
        P("panel", None, None),
    )
    out_specs = (P("mach", "panel", None, None), P("panel", None, None))
    return jax.shard_map(
        on_device, mesh=mesh, in_specs=in_specs, out_specs=out_specs, check_vma=False
    )
```

```python
import jax
import jax.numpy as jnp
from jax import lax
from jax.experimental import pallas as pl
from jax.experimental.pallas import tpu as pltpu
from jax.sharding import PartitionSpec as P

MESH = pl.DeviceIdType.MESH
F32 = jnp.float32
BF16 = jnp.bfloat16
MACHS = 8
PANELS = 64
RING = 8
ROWS = 8
NNZ = 8
TARGETS = 6
RHS = 4
CAP = 2
LANES = TARGETS * ROWS * RHS
SERVED = PANELS // 2
SLOTS = SERVED * CAP * RHS


def iota(shape, axis):
    return lax.broadcasted_iota(jnp.int32, shape, axis)


def ones_where(cond):
    return jnp.where(cond, 1.0, 0.0).astype(BF16)


def kernel(
    adj_hbm,
    near_hbm,
    pat_hbm,
    mask_hbm,
    spline_hbm,
    own_hbm,
    loc_hbm,
    inv_hbm,
    loads_ref,
    struct_ref,
    near_ref,
    spline_ref,
    inv_ref,
    own_ref,
    loc_ref,
    pat_ref,
    mask_ref,
    pool,
    mirror,
    relay,
    near_acc,
    mach_buf,
    place,
    pick,
    tab,
    ytab,
    ycomp,
    ztab,
    send_buf,
    recv_buf,
    load_sem,
    halo_send,
    halo_recv,
    relay_send,
    relay_recv,
    pass_send,
    ring_send,
    ring_recv,
    mach_send,
    mach_recv,
    all_send,
    all_recv,
    core_send,
    core_recv,
    next_ready,
    wrap_ready,
    row_near,
    row_far,
    col_ready,
    mach_ready,
    mach_near,
    mach_far,
    row_in,
):
    m = lax.axis_index("mach")
    p = lax.axis_index("panel")
    z = p // RING
    y = p % RING
    core = m % 2
    barrier = pltpu.get_barrier_semaphore()

    def signal(sem, peer):
        pl.semaphore_signal(sem, inc=1, device_id=peer, device_id_type=MESH)

    def row_peer(j):
        return (m, z * RING + (y + j) % RING)

    def column_peer(j):
        return (m, ((z + j) % RING) * RING + y)

    def mach_peer(j):
        return ((m + j) % MACHS, p)

    half = RING // 2
    x = m // 2
    chips = MACHS // 2
    x_up = ((m + 2) % MACHS, p)
    x_down = ((m + MACHS - 2) % MACHS, p)
    other = (m + 1 - 2 * core, p)
    ends_row = (y == RING - 1) & (z < RING - 1)
    opens_row = (y == 0) & (z > 0)
    row_right = (m, z * RING + (y + 1) % RING)
    row_left = (m, z * RING + (y + RING - 1) % RING)

    @pl.when(x < chips - 1)
    def _():
        signal(barrier, x_up)

    @pl.when(x == 0)
    def _():
        signal(barrier, x_down)

    @pl.when(core == 1)
    def _():
        signal(barrier, other)

    @pl.when(y < half)
    def _():
        signal(barrier, row_right)

    @pl.when((y == 0) | (y > half))
    def _():
        signal(barrier, row_left)

    @pl.when(opens_row & (z != half))
    def _():
        signal(barrier, (m, p - 1))

    @pl.when(ends_row & (z == half - 1))
    def _():
        signal(barrier, (m, p + 1))

    def each(low, high, act):
        def step(k, carry):
            act(k)
            return carry

        lax.fori_loop(low, high, step, 0)

    each(z + 1, RING, lambda k: signal(barrier, (m, k * RING + y)))

    pairs = [
        (adj_hbm, pool.at[pl.ds(ROWS, ROWS)]),
        (own_hbm, own_ref),
        (loc_hbm, loc_ref),
        (pat_hbm, pat_ref),
        (mask_hbm, mask_ref),
        (near_hbm, near_ref),
        (spline_hbm, spline_ref),
        (inv_hbm, inv_ref),
    ]
    loads = [
        pltpu.make_async_copy(src, dst, load_sem.at[n]) for n, (src, dst) in enumerate(pairs)
    ]
    adj_load, own_load, loc_load, pat_load, mask_load, near_load, spline_load, inv_load = loads
    adj_load.start()

    def send(src, dst, send_sem, recv_sem, peer):
        copy = pltpu.make_async_remote_copy(
            src_ref=src,
            dst_ref=dst,
            send_sem=send_sem,
            recv_sem=recv_sem,
            device_id=peer,
            device_id_type=MESH,
        )
        copy.start()
        return copy

    def drain(ref, sem):
        pltpu.make_async_copy(ref, ref, sem).wait()

    row_count = jnp.where(y == 0, 0, jnp.where(y == half, 2, 1))
    later = (ends_row & (z != half - 1)) | (opens_row & (z == half))
    row_count = row_count + later.astype(jnp.int32)
    mach_count = jnp.where(x == 0, 0, jnp.where(x == chips - 1, 2, 1)) + 1 - core
    count = z + mach_count + row_count

    @pl.when(count > 0)
    def _():
        pl.semaphore_wait(barrier, count)

    adj = pool.at[pl.ds(ROWS, ROWS)]
    after_left = ((y > 0) & (y <= half)) | (opens_row & later)
    after_right = ((y >= half) & (y < RING - 1)) | (ends_row & later)
    before_left = (y > half) | (opens_row & jnp.logical_not(later))
    before_right = (y < half) | (ends_row & jnp.logical_not(later))

    @pl.when(z >= RING - 2)
    def _():
        signal(col_ready.at[z], (m, y))

    @pl.when((z == half) | (z == half + 1))
    def _():
        signal(col_ready.at[z], (m, (half - 1) * RING + y))

    @pl.when(after_left)
    def _():
        signal(next_ready.at[1], (m, p - 1))

    @pl.when(after_right)
    def _():
        signal(next_ready.at[0], (m, p + 1))

    @pl.when(z == half - 1)
    def _():
        signal(col_ready.at[z], (m, y))
        signal(col_ready.at[z], (m, RING + y))

    adj_load.wait()

    @pl.when(z >= half)
    def _():
        send(adj, mirror, halo_send.at[0], halo_recv.at[0], (m, p - half * RING))

    def to_left():
        send(adj, pool.at[pl.ds(2 * ROWS, ROWS)], halo_send.at[2], halo_recv.at[2], (m, p - 1))

    def to_right():
        send(adj, pool.at[pl.ds(0, ROWS)], halo_send.at[1], halo_recv.at[1], (m, p + 1))

    pl.when(after_left)(to_left)
    pl.when(after_right)(to_right)

    for copy in loads[1:]:
        copy.start()

    @pl.when(y == RING - 1)
    def _():
        signal(wrap_ready, row_right)

    @pl.when(core == 0)
    def _():
        signal(mach_ready, other)

    @pl.when(x > 0)
    def _():
        signal(mach_ready, x_down)

    @pl.when(x == chips - 1)
    def _():
        signal(mach_ready, x_up)

    def answer(k):
        told = (
            (z >= RING - 2) & (k == 0)
            | ((z == half) | (z == half + 1)) & (k == half - 1)
            | (z == half - 1) & (k < 2)
        )

        @pl.when(jnp.logical_not(told))
        def _():
            signal(col_ready.at[z], (m, k * RING + y))

    each(0, z, answer)

    @pl.when((z >= 2) & (z < half))
    def _():
        send(adj, relay.at[z - 2], halo_send.at[0], relay_recv.at[z - 2], (m, p - z * RING))

    @pl.when(before_left)
    def _():
        pl.semaphore_wait(next_ready.at[0], 1)
        to_left()

    @pl.when(before_right)
    def _():
        pl.semaphore_wait(next_ready.at[1], 1)
        to_right()

    @pl.when(z < 2)
    def _():
        pl.semaphore_wait(col_ready.at[half - 1], 1)
        send(
            adj, relay.at[z], halo_send.at[0], relay_recv.at[z], (m, p + (half - 1 - z) * RING)
        )

    @pl.when(y == 0)
    def _():
        pl.semaphore_wait(wrap_ready, 1)

    @pl.when(mach_count < 3)
    def _():
        pl.semaphore_wait(mach_ready, 3 - mach_count)

    signal(mach_near, x_up)
    signal(mach_near, x_down)
    signal(mach_near, other)
    signal(row_near, row_right)
    signal(row_near, row_left)

    own_load.wait()
    loc_load.wait()
    own = own_ref[...].astype(F32)
    loc = loc_ref[...].astype(F32)
    lane = iota((ROWS, LANES), 1)
    sub = iota((ROWS, LANES), 0)
    lane_s = lane // (ROWS * RHS)
    lane_i = (lane // RHS) % ROWS
    own_rows = jnp.zeros((ROWS, LANES), F32)
    loc_rows = jnp.zeros((ROWS, LANES), F32)
    for s in range(TARGETS):
        own_rows = jnp.where(lane_s == s, own[:, s : s + 1], own_rows)
        loc_rows = jnp.where(lane_s == s, loc[:, s : s + 1], loc_rows)
    mine = sub == lane_i
    own_lane = jnp.sum(jnp.where(mine, own_rows, 0.0), axis=0, keepdims=True)
    loc_lane = jnp.sum(jnp.where(mine, loc_rows, 0.0), axis=0, keepdims=True)
    same = jnp.zeros((ROWS, LANES), F32)
    for s in range(TARGETS):
        same = same + jnp.where(own[:, s : s + 1] == own_lane, 1.0, 0.0)
    slot = jnp.sum(jnp.where(sub < lane_i, same, 0.0), axis=0, keepdims=True)
    dest = own_lane * CAP + slot
    lane_r = (iota((1, LANES), 1) % RHS).astype(F32)
    chosen = ones_where(iota((PANELS * CAP, LANES), 0).astype(F32) == dest)
    weights = jnp.broadcast_to(
        jnp.where(lane_r == 0.0, loc_lane + 1.0, 0.0), (ROWS, LANES)
    ).astype(BF16)
    tab[...] = lax.dot_general(
        weights, chosen, (((1,), (1,)), ((), ())), preferred_element_type=F32
    )[:1]

    owner_row = iota((SLOTS, LANES), 0)
    owner_row = (owner_row // (CAP * RHS)) * (2 * CAP * RHS) + owner_row % (CAP * RHS)
    owner_row = owner_row + core * (CAP * RHS)
    place[...] = ones_where(owner_row.astype(F32) == dest * RHS + lane_r)

    def pass_on(slot, child):
        pltpu.make_async_copy(relay.at[slot], relay.at[slot], relay_recv.at[slot]).wait()
        pl.semaphore_wait(col_ready.at[child], 1)
        send(
            relay.at[slot], mirror, pass_send.at[slot], halo_recv.at[0], (m, child * RING + y)
        )

    @pl.when(z == 3)
    def _():
        pass_on(0, 4)
        pass_on(1, 5)

    @pl.when(z == 0)
    def _():
        pass_on(0, 6)
        pass_on(1, 7)

    pl.semaphore_wait(mach_near, 3)
    signal(mach_far, other)
    pl.semaphore_wait(row_near, 2)
    for j in (1, 2, RING - 2, RING - 1):
        signal(row_far, row_peer(j))

    pat_load.wait()
    near_load.wait()

    @pl.when(p > 0)
    def _():
        drain(mirror, halo_recv.at[1])

    @pl.when(p < PANELS - 1)
    def _():
        drain(mirror, halo_recv.at[2])

    for i in range(ROWS):
        picked = [
            pool[jnp.clip(pat_ref[i, k] - p * ROWS + ROWS, 0, 3 * ROWS - 1)]
            for k in range(2, NNZ)
        ]
        near_acc[RHS * i : RHS * (i + 1), :] = jnp.dot(
            pool[ROWS + i], near_ref[i, 0], preferred_element_type=F32
        ) + jnp.dot(
            jnp.concatenate(picked, axis=1),
            near_ref[i, 2:NNZ].reshape((NNZ - 2) * 128, 128),
            preferred_element_type=F32,
        )

    mask_load.wait()
    row32 = iota((ROWS * RHS, 1), 0)
    gate = jnp.zeros((ROWS * RHS, 1), F32)
    for r in range(RHS):
        gate = jnp.where(row32 % RHS == r, mask_ref[0, r].astype(F32), gate)

    pl.semaphore_wait(row_far, 4)
    for j in range(1, RING):
        send(tab, ytab.at[y], ring_send.at[0], ring_recv.at[0], row_peer(j))
    ytab[y] = tab[...]

    for k in range(1, RING):
        early = (z == 0) & (k in (3, 6, 7)) | (z == 1) & (k == 3) | (z == 3) & (k in (4, 5))

        @pl.when((k > z) & jnp.logical_not(early))
        def _():
            pl.semaphore_wait(col_ready.at[k], 1)

    for j in range(1, RING):
        signal(row_in, column_peer(j))

    pl.semaphore_wait(mach_far, 1)
    drain(mirror, halo_recv.at[0])
    for i in range(ROWS):
        near_acc[RHS * i : RHS * (i + 1), :] += jnp.dot(
            mirror[i], near_ref[i, 1], preferred_element_type=F32
        )
    masked = near_acc[...] * gate
    mach_buf[m] = masked.astype(BF16)
    for j in (4, 3, 5, 2, 6, 1, 7):
        send(mach_buf.at[m], mach_buf.at[m], mach_send, mach_recv, mach_peer(j))
    loads_ref[...] = masked

    spline_load.wait()
    drain(mach_buf.at[pl.ds(0, MACHS - 1)], mach_recv)
    total = mach_buf[0].astype(F32)
    for j in range(1, MACHS):
        total = total + mach_buf[j].astype(F32)
    high = total.astype(BF16).astype(F32)
    both = jnp.concatenate([high, total - high], axis=0)
    row64 = (iota((2 * ROWS * RHS, 128), 0) // RHS) % ROWS
    spread = jnp.concatenate(
        [jnp.where(row64 == i, both, 0.0).astype(BF16) for i in range(ROWS)], axis=1
    )
    contrib = []
    for s in range(TARGETS):
        out = jnp.dot(
            spread,
            spline_ref[:, s].reshape(ROWS * 128, 128),
            preferred_element_type=F32,
        )
        contrib.append((out[: ROWS * RHS] + out[ROWS * RHS :]).astype(BF16))
    packed = jnp.dot(
        place[...], jnp.concatenate(contrib, axis=0), preferred_element_type=F32
    )
    send_buf[...] = packed.astype(BF16).reshape(SERVED, CAP * RHS, 128)

    serves = y % 2 == core
    pl.semaphore_wait(row_in, RING - 1)

    def post(j, carry):
        far = j // (RING // 2)
        side = 1 - 2 * (far % 2)
        to_z = (z + RING // 2 + side * ((far + 1) // 2) + RING) % RING
        to_y = ((y // 2 + 2 + j % (RING // 2)) % (RING // 2)) * 2 + core
        peer = to_z * RING + to_y

        @pl.when(peer != p)
        def _():
            send(send_buf.at[peer // 2], recv_buf.at[p], all_send, all_recv, (m, peer))

        return carry

    lax.fori_loop(0, SERVED, post, 0)

    drain(ytab.at[pl.ds(0, RING - 1)], ring_recv.at[0])
    sub8 = iota((RING, 128), 0)
    comp = jnp.zeros((RING, 128), F32)
    for j in range(RING):
        comp = jnp.where(sub8 == j, ytab[j], comp)
    ycomp[...] = comp.astype(BF16)
    for j in range(1, RING):
        send(ycomp, ztab.at[z], ring_send.at[1], ring_recv.at[1], column_peer(j))
    ztab[z] = ycomp[...]

    drain(ztab.at[pl.ds(0, RING - 1)], ring_recv.at[1])
    inv_load.wait()

    @pl.when(serves)
    def _():
        recv_buf[p] = send_buf[p // 2]
        lane5 = iota((128, PANELS * CAP * RHS), 1)
        wanted = ones_where(iota((128, PANELS * CAP * RHS), 0) == p * CAP + (lane5 // RHS) % CAP)
        blocks = jnp.dot(
            ztab[...].astype(F32).reshape(PANELS, 128).astype(BF16), wanted, preferred_element_type=F32
        )
        shape = (PANELS, PANELS * CAP * RHS)
        from_panel = iota(shape, 0) == iota(shape, 1) // (CAP * RHS)
        block_lane = jnp.sum(jnp.where(from_panel, blocks, 0.0), axis=0, keepdims=True)
        shape = (ROWS * RHS, PANELS * CAP * RHS)
        row5 = iota(shape, 0)
        col5 = iota(shape, 1)
        pick[...] = ones_where(
            (block_lane == (row5 // RHS + 1).astype(F32)) & (col5 % RHS == row5 % RHS)
        )
        drain(recv_buf.at[pl.ds(0, PANELS - 1)], all_recv)
        found = jnp.dot(
            pick[...],
            recv_buf[...].reshape(PANELS * CAP * RHS, 128),
            preferred_element_type=F32,
        )
        row_block = iota((ROWS * RHS, 128), 0) // RHS
        wide = jnp.concatenate(
            [jnp.where(row_block == t, found, 0.0).astype(BF16) for t in range(ROWS)], axis=1
        )
        struct_ref[...] = jnp.dot(
            wide, inv_ref[...].reshape(ROWS * 128, 128), preferred_element_type=F32
        )
        send(struct_ref, struct_ref, core_send, core_recv, other)
        drain(send_buf.at[pl.ds(0, SERVED - 1)], all_send)
        drain(struct_ref, core_send)

    @pl.when(jnp.logical_not(serves))
    def _():
        drain(send_buf, all_send)
        drain(struct_ref, core_recv)

    drain(mirror, halo_send.at[0])

    @pl.when(p < PANELS - 1)
    def _():
        drain(mirror, halo_send.at[1])

    @pl.when(p > 0)
    def _():
        drain(mirror, halo_send.at[2])

    @pl.when((z == 0) | (z == 3))
    def _():
        drain(mirror, pass_send.at[0])
        drain(mirror, pass_send.at[1])

    for stage, ref in enumerate((ytab, ztab)):
        drain(ref.at[pl.ds(0, RING - 1)], ring_send.at[stage])
    drain(mach_buf.at[pl.ds(0, MACHS - 1)], mach_send)


def hand_on(loads_ref, struct_ref, loads_out, struct_out):
    loads_out[...] = loads_ref[...]
    struct_out[...] = struct_ref[...]


def on_device(adjoint, near, pattern, mask, spline, owner, local, inverse):
    vmem = pl.BlockSpec(memory_space=pltpu.VMEM)
    hbm = pl.BlockSpec(memory_space=pl.ANY)
    rows = ROWS * RHS
    dma = pltpu.SemaphoreType.DMA
    regular = pltpu.SemaphoreType.REGULAR
    loads, struct = pl.pallas_call(
        kernel,
        out_shape=(
            pltpu.VMEM((rows, 128), F32),
            pltpu.VMEM((rows, 128), F32),
        ),
        in_specs=[hbm] * 8,
        out_specs=(vmem, vmem),
        scratch_shapes=[
            pltpu.VMEM((ROWS, NNZ, 128, 128), BF16),
            pltpu.VMEM((ROWS, TARGETS, 128, 128), BF16),
            pltpu.VMEM((ROWS, 128, 128), BF16),
            pltpu.VMEM((ROWS, TARGETS), jnp.int32),
            pltpu.VMEM((ROWS, TARGETS), jnp.int32),
            pltpu.SMEM((ROWS, NNZ), jnp.int32),
            pltpu.SMEM((1, RHS), jnp.int32),
            pltpu.VMEM((3 * ROWS, RHS, 128), BF16),
            pltpu.VMEM((ROWS, RHS, 128), BF16),
            pltpu.VMEM((2, ROWS, RHS, 128), BF16),
            pltpu.VMEM((rows, 128), F32),
            pltpu.VMEM((MACHS, rows, 128), BF16),
            pltpu.VMEM((SLOTS, LANES), BF16),
            pltpu.VMEM((rows, PANELS * CAP * RHS), BF16),
            pltpu.VMEM((1, 128), F32),
            pltpu.VMEM((RING, 1, 128), F32),
            pltpu.VMEM((RING, 128), BF16),
            pltpu.VMEM((RING, RING, 128), BF16),
            pltpu.VMEM((SERVED, CAP * RHS, 128), BF16),
            pltpu.VMEM((PANELS, CAP * RHS, 128), BF16),
            dma((8,)),
            dma((3,)),
            dma((3,)),
            dma((2,)),
            dma((2,)),
            dma((2,)),
            dma((2,)),
            dma((2,)),
            dma,
            dma,
            dma,
            dma,
            dma,
            dma,
            regular((2,)),
            regular,
            regular,
            regular,
            regular((RING,)),
            regular,
            regular,
            regular,
            regular,
        ],
        compiler_params=pltpu.CompilerParams(collective_id=0, has_side_effects=True),
        name="load_transfer",
    )(adjoint[0], near[0], pattern, mask, spline, owner, local, inverse)
    out = jax.ShapeDtypeStruct((rows, 128), F32)
    loads, struct = pl.pallas_call(
        hand_on,
        out_shape=(out, out),
        in_specs=[vmem, vmem],
        out_specs=(vmem, vmem),
        name="hand_on",
        compiler_params=pltpu.CompilerParams(vmem_limit_bytes=1 << 20),
    )(loads, struct)
    return loads.reshape(1, ROWS, RHS, 128), struct.reshape(ROWS, RHS, 128)


def solution(mesh):
    in_specs = (
        P("mach", "panel", None, None),
        P("mach", "panel", None, None, None),
        P("panel", None),
        P("mach", None),
        P("panel", None, None, None),
        P("panel", None),
        P("panel", None),
        P("panel", None, None),
    )
    out_specs = (P("mach", "panel", None, None), P("panel", None, None))
    return jax.shard_map(
        on_device, mesh=mesh, in_specs=in_specs, out_specs=out_specs, check_vma=False
    )
```

```python
import jax
import jax.numpy as jnp
from jax import lax
from jax.experimental import pallas as pl
from jax.experimental.pallas import tpu as pltpu
from jax.sharding import PartitionSpec as P

MESH = pl.DeviceIdType.MESH
F32 = jnp.float32
BF16 = jnp.bfloat16
MACHS = 8
PANELS = 64
RING = 8
ROWS = 8
NNZ = 8
TARGETS = 6
RHS = 4
CAP = 2
LANES = TARGETS * ROWS * RHS
SERVED = PANELS // 2
SLOTS = SERVED * CAP * RHS


def iota(shape, axis):
    return lax.broadcasted_iota(jnp.int32, shape, axis)


def ones_where(cond):
    return jnp.where(cond, 1.0, 0.0).astype(BF16)


def kernel(
    adj_hbm,
    near_hbm,
    pat_hbm,
    mask_hbm,
    spline_hbm,
    own_hbm,
    loc_hbm,
    inv_hbm,
    loads_ref,
    struct_ref,
    near_ref,
    spline_ref,
    inv_ref,
    own_ref,
    loc_ref,
    pat_ref,
    mask_ref,
    pool,
    mirror,
    relay,
    near_acc,
    mach_buf,
    place,
    pick,
    tab,
    ytab,
    ycomp,
    ztab,
    send_buf,
    recv_buf,
    load_sem,
    halo_send,
    halo_recv,
    relay_send,
    relay_recv,
    pass_send,
    ring_send,
    ring_recv,
    mach_send,
    mach_recv,
    all_send,
    both_send,
    all_recv,
    core_send,
    core_recv,
    next_ready,
    wrap_ready,
    row_near,
    row_far,
    col_ready,
    mach_ready,
    mach_near,
    mach_far,
    row_in,
):
    m = lax.axis_index("mach")
    p = lax.axis_index("panel")
    z = p // RING
    y = p % RING
    core = m % 2
    parity = 1 - core
    barrier = pltpu.get_barrier_semaphore()

    def signal(sem, peer):
        pl.semaphore_signal(sem, inc=1, device_id=peer, device_id_type=MESH)

    def row_peer(j):
        return (m, z * RING + (y + j) % RING)

    def column_peer(j):
        return (m, ((z + j) % RING) * RING + y)

    def mach_peer(j):
        return ((m + j) % MACHS, p)

    half = RING // 2
    x = m // 2
    chips = MACHS // 2
    x_up = ((m + 2) % MACHS, p)
    x_down = ((m + MACHS - 2) % MACHS, p)
    other = (m + 1 - 2 * core, p)
    ends_row = (y == RING - 1) & (z < RING - 1)
    opens_row = (y == 0) & (z > 0)
    row_right = (m, z * RING + (y + 1) % RING)
    row_left = (m, z * RING + (y + RING - 1) % RING)

    @pl.when(x < chips - 1)
    def _():
        signal(barrier, x_up)

    @pl.when(x == 0)
    def _():
        signal(barrier, x_down)

    @pl.when(core == 1)
    def _():
        signal(barrier, other)

    @pl.when(y < half)
    def _():
        signal(barrier, row_right)

    @pl.when((y == 0) | (y > half))
    def _():
        signal(barrier, row_left)

    @pl.when(opens_row & (z != half))
    def _():
        signal(barrier, (m, p - 1))

    @pl.when(ends_row & (z == half - 1))
    def _():
        signal(barrier, (m, p + 1))

    def each(low, high, act):
        def step(k, carry):
            act(k)
            return carry

        lax.fori_loop(low, high, step, 0)

    each(z + 1, RING, lambda k: signal(barrier, (m, k * RING + y)))

    pairs = [
        (adj_hbm, pool.at[pl.ds(ROWS, ROWS)]),
        (own_hbm, own_ref),
        (loc_hbm, loc_ref),
        (pat_hbm, pat_ref),
        (mask_hbm, mask_ref),
        (near_hbm, near_ref),
        (spline_hbm, spline_ref),
        (inv_hbm, inv_ref),
    ]
    loads = [
        pltpu.make_async_copy(src, dst, load_sem.at[n]) for n, (src, dst) in enumerate(pairs)
    ]
    adj_load, own_load, loc_load, pat_load, mask_load, near_load, spline_load, inv_load = loads
    adj_load.start()

    def send(src, dst, send_sem, recv_sem, peer):
        copy = pltpu.make_async_remote_copy(
            src_ref=src,
            dst_ref=dst,
            send_sem=send_sem,
            recv_sem=recv_sem,
            device_id=peer,
            device_id_type=MESH,
        )
        copy.start()
        return copy

    def drain(ref, sem):
        pltpu.make_async_copy(ref, ref, sem).wait()

    row_count = jnp.where(y == 0, 0, jnp.where(y == half, 2, 1))
    later = (ends_row & (z != half - 1)) | (opens_row & (z == half))
    row_count = row_count + later.astype(jnp.int32)
    mach_count = jnp.where(x == 0, 0, jnp.where(x == chips - 1, 2, 1)) + 1 - core
    count = z + mach_count + row_count

    @pl.when(count > 0)
    def _():
        pl.semaphore_wait(barrier, count)

    adj = pool.at[pl.ds(ROWS, ROWS)]
    after_left = ((y > 0) & (y <= half)) | (opens_row & later)
    after_right = ((y >= half) & (y < RING - 1)) | (ends_row & later)
    before_left = (y > half) | (opens_row & jnp.logical_not(later))
    before_right = (y < half) | (ends_row & jnp.logical_not(later))

    @pl.when(z >= RING - 2)
    def _():
        signal(col_ready.at[z], (m, y))

    @pl.when((z == half) | (z == half + 1))
    def _():
        signal(col_ready.at[z], (m, (half - 1) * RING + y))

    @pl.when(after_left)
    def _():
        signal(next_ready.at[1], (m, p - 1))

    @pl.when(after_right)
    def _():
        signal(next_ready.at[0], (m, p + 1))

    @pl.when(z == half - 1)
    def _():
        signal(col_ready.at[z], (m, y))
        signal(col_ready.at[z], (m, RING + y))

    adj_load.wait()

    @pl.when(z >= half)
    def _():
        send(adj, mirror, halo_send.at[0], halo_recv.at[0], (m, p - half * RING))

    def to_left():
        send(adj, pool.at[pl.ds(2 * ROWS, ROWS)], halo_send.at[2], halo_recv.at[2], (m, p - 1))

    def to_right():
        send(adj, pool.at[pl.ds(0, ROWS)], halo_send.at[1], halo_recv.at[1], (m, p + 1))

    pl.when(after_left)(to_left)
    pl.when(after_right)(to_right)

    for copy in loads[1:]:
        copy.start()

    @pl.when(y == RING - 1)
    def _():
        signal(wrap_ready, row_right)

    @pl.when(core == 0)
    def _():
        signal(mach_ready, other)

    @pl.when(x > 0)
    def _():
        signal(mach_ready, x_down)

    @pl.when(x == chips - 1)
    def _():
        signal(mach_ready, x_up)

    def answer(k):
        told = (
            (z >= RING - 2) & (k == 0)
            | ((z == half) | (z == half + 1)) & (k == half - 1)
            | (z == half - 1) & (k < 2)
        )

        @pl.when(jnp.logical_not(told))
        def _():
            signal(col_ready.at[z], (m, k * RING + y))

    each(0, z, answer)

    @pl.when((z >= 2) & (z < half))
    def _():
        send(adj, relay.at[z - 2], halo_send.at[0], relay_recv.at[z - 2], (m, p - z * RING))

    @pl.when(before_left)
    def _():
        pl.semaphore_wait(next_ready.at[0], 1)
        to_left()

    @pl.when(before_right)
    def _():
        pl.semaphore_wait(next_ready.at[1], 1)
        to_right()

    @pl.when(z < 2)
    def _():
        pl.semaphore_wait(col_ready.at[half - 1], 1)
        send(
            adj, relay.at[z], halo_send.at[0], relay_recv.at[z], (m, p + (half - 1 - z) * RING)
        )

    @pl.when(y == 0)
    def _():
        pl.semaphore_wait(wrap_ready, 1)

    @pl.when(mach_count < 3)
    def _():
        pl.semaphore_wait(mach_ready, 3 - mach_count)

    signal(mach_near, x_up)
    signal(mach_near, x_down)
    signal(mach_near, other)
    signal(row_near, row_right)
    signal(row_near, row_left)

    own_load.wait()
    loc_load.wait()
    own = own_ref[...].astype(F32)
    loc = loc_ref[...].astype(F32)
    lane = iota((ROWS, LANES), 1)
    sub = iota((ROWS, LANES), 0)
    lane_s = lane // (ROWS * RHS)
    lane_i = (lane // RHS) % ROWS
    own_rows = jnp.zeros((ROWS, LANES), F32)
    loc_rows = jnp.zeros((ROWS, LANES), F32)
    for s in range(TARGETS):
        own_rows = jnp.where(lane_s == s, own[:, s : s + 1], own_rows)
        loc_rows = jnp.where(lane_s == s, loc[:, s : s + 1], loc_rows)
    mine = sub == lane_i
    own_lane = jnp.sum(jnp.where(mine, own_rows, 0.0), axis=0, keepdims=True)
    loc_lane = jnp.sum(jnp.where(mine, loc_rows, 0.0), axis=0, keepdims=True)
    same = jnp.zeros((ROWS, LANES), F32)
    for s in range(TARGETS):
        same = same + jnp.where(own[:, s : s + 1] == own_lane, 1.0, 0.0)
    slot = jnp.sum(jnp.where(sub < lane_i, same, 0.0), axis=0, keepdims=True)
    dest = own_lane * CAP + slot
    lane_r = (iota((1, LANES), 1) % RHS).astype(F32)
    chosen = ones_where(iota((PANELS * CAP, LANES), 0).astype(F32) == dest)
    weights = jnp.broadcast_to(
        jnp.where(lane_r == 0.0, loc_lane + 1.0, 0.0), (ROWS, LANES)
    ).astype(BF16)
    tab[...] = lax.dot_general(
        weights, chosen, (((1,), (1,)), ((), ())), preferred_element_type=F32
    )[:1]

    owner_row = iota((SLOTS, LANES), 0)
    owner_row = (owner_row // (CAP * RHS)) * (2 * CAP * RHS) + owner_row % (CAP * RHS)
    owner_row = owner_row + parity * (CAP * RHS)
    place[...] = ones_where(owner_row.astype(F32) == dest * RHS + lane_r)

    def pass_on(slot, child):
        pltpu.make_async_copy(relay.at[slot], relay.at[slot], relay_recv.at[slot]).wait()
        pl.semaphore_wait(col_ready.at[child], 1)
        send(
            relay.at[slot], mirror, pass_send.at[slot], halo_recv.at[0], (m, child * RING + y)
        )

    @pl.when(z == 3)
    def _():
        pass_on(0, 4)
        pass_on(1, 5)

    @pl.when(z == 0)
    def _():
        pass_on(0, 6)
        pass_on(1, 7)

    pl.semaphore_wait(mach_near, 3)
    signal(mach_far, other)
    pl.semaphore_wait(row_near, 2)
    for j in (1, 2, RING - 2, RING - 1):
        signal(row_far, row_peer(j))

    pat_load.wait()
    near_load.wait()

    @pl.when(p > 0)
    def _():
        drain(mirror, halo_recv.at[1])

    @pl.when(p < PANELS - 1)
    def _():
        drain(mirror, halo_recv.at[2])

    for i in range(ROWS):
        picked = [
            pool[jnp.clip(pat_ref[i, k] - p * ROWS + ROWS, 0, 3 * ROWS - 1)]
            for k in range(2, NNZ)
        ]
        near_acc[RHS * i : RHS * (i + 1), :] = jnp.dot(
            pool[ROWS + i], near_ref[i, 0], preferred_element_type=F32
        ) + jnp.dot(
            jnp.concatenate(picked, axis=1),
            near_ref[i, 2:NNZ].reshape((NNZ - 2) * 128, 128),
            preferred_element_type=F32,
        )

    mask_load.wait()
    row32 = iota((ROWS * RHS, 1), 0)
    gate = jnp.zeros((ROWS * RHS, 1), F32)
    for r in range(RHS):
        gate = jnp.where(row32 % RHS == r, mask_ref[0, r].astype(F32), gate)

    pl.semaphore_wait(row_far, 4)
    for j in range(1, RING):
        send(tab, ytab.at[y], ring_send.at[0], ring_recv.at[0], row_peer(j))
    ytab[y] = tab[...]

    for k in range(1, RING):
        early = (z == 0) & (k in (3, 6, 7)) | (z == 1) & (k == 3) | (z == 3) & (k in (4, 5))

        @pl.when((k > z) & jnp.logical_not(early))
        def _():
            pl.semaphore_wait(col_ready.at[k], 1)

    for j in range(1, RING):
        signal(row_in, column_peer(j))

    pl.semaphore_wait(mach_far, 1)
    drain(mirror, halo_recv.at[0])
    for i in range(ROWS):
        near_acc[RHS * i : RHS * (i + 1), :] += jnp.dot(
            mirror[i], near_ref[i, 1], preferred_element_type=F32
        )
    masked = near_acc[...] * gate
    mach_buf[m] = masked.astype(BF16)
    for j in (4, 3, 5, 2, 6, 1, 7):
        send(mach_buf.at[m], mach_buf.at[m], mach_send, mach_recv, mach_peer(j))
    loads_ref[...] = masked

    spline_load.wait()
    drain(mach_buf.at[pl.ds(0, MACHS - 1)], mach_recv)
    total = mach_buf[0].astype(F32)
    for j in range(1, MACHS):
        total = total + mach_buf[j].astype(F32)
    high = total.astype(BF16).astype(F32)
    both = jnp.concatenate([high, total - high], axis=0)
    row64 = (iota((2 * ROWS * RHS, 128), 0) // RHS) % ROWS
    spread = jnp.concatenate(
        [jnp.where(row64 == i, both, 0.0).astype(BF16) for i in range(ROWS)], axis=1
    )
    contrib = []
    for s in range(TARGETS):
        out = jnp.dot(
            spread,
            spline_ref[:, s].reshape(ROWS * 128, 128),
            preferred_element_type=F32,
        )
        contrib.append((out[: ROWS * RHS] + out[ROWS * RHS :]).astype(BF16))
    packed = jnp.dot(
        place[...], jnp.concatenate(contrib, axis=0), preferred_element_type=F32
    )
    send_buf[...] = packed.astype(BF16).reshape(SERVED, CAP * RHS, 128)

    serves = y % 2 == parity
    first = p == 0
    pl.semaphore_wait(row_in, RING - 1)

    def post(j, carry):
        far = j // (RING // 2)
        side = 1 - 2 * (far % 2)
        to_z = (z + RING // 2 + side * ((far + 1) // 2) + RING) % RING
        to_y = ((y // 2 + 2 + j % (RING // 2)) % (RING // 2)) * 2 + parity
        peer = to_z * RING + to_y

        @pl.when((peer != p) & (peer != 0))
        def _():
            send(send_buf.at[peer // 2], recv_buf.at[p], all_send, all_recv, (m, peer))

        return carry

    @pl.when(parity == 0)
    def _():
        send(send_buf.at[0], recv_buf.at[p], both_send, all_recv, (m - 1, 0))

        @pl.when(p > 0)
        def _():
            send(send_buf.at[0], recv_buf.at[p], all_send, all_recv, (m, 0))

    lax.fori_loop(0, SERVED, post, 0)

    drain(ytab.at[pl.ds(0, RING - 1)], ring_recv.at[0])
    sub8 = iota((RING, 128), 0)
    comp = jnp.zeros((RING, 128), F32)
    for j in range(RING):
        comp = jnp.where(sub8 == j, ytab[j], comp)
    ycomp[...] = comp.astype(BF16)
    for j in range(1, RING):
        send(ycomp, ztab.at[z], ring_send.at[1], ring_recv.at[1], column_peer(j))
    ztab[z] = ycomp[...]

    drain(ztab.at[pl.ds(0, RING - 1)], ring_recv.at[1])
    inv_load.wait()

    @pl.when(serves)
    def _():
        recv_buf[p] = send_buf[p // 2]

    @pl.when(serves | first)
    def _():
        lane5 = iota((128, PANELS * CAP * RHS), 1)
        wanted = ones_where(iota((128, PANELS * CAP * RHS), 0) == p * CAP + (lane5 // RHS) % CAP)
        blocks = jnp.dot(
            ztab[...].astype(F32).reshape(PANELS, 128).astype(BF16), wanted, preferred_element_type=F32
        )
        shape = (PANELS, PANELS * CAP * RHS)
        from_panel = iota(shape, 0) == iota(shape, 1) // (CAP * RHS)
        block_lane = jnp.sum(jnp.where(from_panel, blocks, 0.0), axis=0, keepdims=True)
        shape = (ROWS * RHS, PANELS * CAP * RHS)
        row5 = iota(shape, 0)
        col5 = iota(shape, 1)
        pick[...] = ones_where(
            (block_lane == (row5 // RHS + 1).astype(F32)) & (col5 % RHS == row5 % RHS)
        )

        @pl.when(serves)
        def _():
            drain(recv_buf.at[pl.ds(0, PANELS - 1)], all_recv)

        @pl.when(jnp.logical_not(serves))
        def _():
            drain(recv_buf, all_recv)

        found = jnp.dot(
            pick[...],
            recv_buf[...].reshape(PANELS * CAP * RHS, 128),
            preferred_element_type=F32,
        )
        row_block = iota((ROWS * RHS, 128), 0) // RHS
        wide = jnp.concatenate(
            [jnp.where(row_block == t, found, 0.0).astype(BF16) for t in range(ROWS)], axis=1
        )
        struct_ref[...] = jnp.dot(
            wide, inv_ref[...].reshape(ROWS * 128, 128), preferred_element_type=F32
        )

    alone = jnp.logical_not(first)

    @pl.when(serves & alone)
    def _():
        send(struct_ref, struct_ref, core_send, core_recv, other)
        drain(struct_ref, core_send)

    @pl.when(jnp.logical_not(serves) & alone)
    def _():
        drain(struct_ref, core_recv)

    @pl.when(serves)
    def _():
        drain(send_buf.at[pl.ds(0, SERVED - 1)], all_send)

    @pl.when(jnp.logical_not(serves))
    def _():
        drain(send_buf, all_send)

    @pl.when(parity == 0)
    def _():
        drain(send_buf.at[pl.ds(0, 1)], both_send)

    drain(mirror, halo_send.at[0])

    @pl.when(p < PANELS - 1)
    def _():
        drain(mirror, halo_send.at[1])

    @pl.when(p > 0)
    def _():
        drain(mirror, halo_send.at[2])

    @pl.when((z == 0) | (z == 3))
    def _():
        drain(mirror, pass_send.at[0])
        drain(mirror, pass_send.at[1])

    for stage, ref in enumerate((ytab, ztab)):
        drain(ref.at[pl.ds(0, RING - 1)], ring_send.at[stage])
    drain(mach_buf.at[pl.ds(0, MACHS - 1)], mach_send)


def hand_on(loads_ref, struct_ref, loads_out, struct_out):
    loads_out[...] = loads_ref[...]
    struct_out[...] = struct_ref[...]


def on_device(adjoint, near, pattern, mask, spline, owner, local, inverse):
    vmem = pl.BlockSpec(memory_space=pltpu.VMEM)
    hbm = pl.BlockSpec(memory_space=pl.ANY)
    rows = ROWS * RHS
    dma = pltpu.SemaphoreType.DMA
    regular = pltpu.SemaphoreType.REGULAR
    loads, struct = pl.pallas_call(
        kernel,
        out_shape=(
            pltpu.VMEM((rows, 128), F32),
            pltpu.VMEM((rows, 128), F32),
        ),
        in_specs=[hbm] * 8,
        out_specs=(vmem, vmem),
        scratch_shapes=[
            pltpu.VMEM((ROWS, NNZ, 128, 128), BF16),
            pltpu.VMEM((ROWS, TARGETS, 128, 128), BF16),
            pltpu.VMEM((ROWS, 128, 128), BF16),
            pltpu.VMEM((ROWS, TARGETS), jnp.int32),
            pltpu.VMEM((ROWS, TARGETS), jnp.int32),
            pltpu.SMEM((ROWS, NNZ), jnp.int32),
            pltpu.SMEM((1, RHS), jnp.int32),
            pltpu.VMEM((3 * ROWS, RHS, 128), BF16),
            pltpu.VMEM((ROWS, RHS, 128), BF16),
            pltpu.VMEM((2, ROWS, RHS, 128), BF16),
            pltpu.VMEM((rows, 128), F32),
            pltpu.VMEM((MACHS, rows, 128), BF16),
            pltpu.VMEM((SLOTS, LANES), BF16),
            pltpu.VMEM((rows, PANELS * CAP * RHS), BF16),
            pltpu.VMEM((1, 128), F32),
            pltpu.VMEM((RING, 1, 128), F32),
            pltpu.VMEM((RING, 128), BF16),
            pltpu.VMEM((RING, RING, 128), BF16),
            pltpu.VMEM((SERVED, CAP * RHS, 128), BF16),
            pltpu.VMEM((PANELS, CAP * RHS, 128), BF16),
            dma((8,)),
            dma((3,)),
            dma((3,)),
            dma((2,)),
            dma((2,)),
            dma((2,)),
            dma((2,)),
            dma((2,)),
            dma,
            dma,
            dma,
            dma,
            dma,
            dma,
            dma,
            regular((2,)),
            regular,
            regular,
            regular,
            regular((RING,)),
            regular,
            regular,
            regular,
            regular,
        ],
        compiler_params=pltpu.CompilerParams(collective_id=0, has_side_effects=True),
        name="load_transfer",
    )(adjoint[0], near[0], pattern, mask, spline, owner, local, inverse)
    out = jax.ShapeDtypeStruct((rows, 128), F32)
    loads, struct = pl.pallas_call(
        hand_on,
        out_shape=(out, out),
        in_specs=[vmem, vmem],
        out_specs=(vmem, vmem),
        name="hand_on",
        compiler_params=pltpu.CompilerParams(vmem_limit_bytes=1 << 20),
    )(loads, struct)
    return loads.reshape(1, ROWS, RHS, 128), struct.reshape(ROWS, RHS, 128)


def solution(mesh):
    in_specs = (
        P("mach", "panel", None, None),
        P("mach", "panel", None, None, None),
        P("panel", None),
        P("mach", None),
        P("panel", None, None, None),
        P("panel", None),
        P("panel", None),
        P("panel", None, None),
    )
    out_specs = (P("mach", "panel", None, None), P("panel", None, None))
    return jax.shard_map(
        on_device, mesh=mesh, in_specs=in_specs, out_specs=out_specs, check_vma=False
    )
```

```python
import jax
import jax.numpy as jnp
from jax import lax
from jax.experimental import pallas as pl
from jax.experimental.pallas import tpu as pltpu
from jax.sharding import PartitionSpec as P

MESH = pl.DeviceIdType.MESH
F32 = jnp.float32
BF16 = jnp.bfloat16
MACHS = 8
PANELS = 64
RING = 8
ROWS = 8
NNZ = 8
TARGETS = 6
RHS = 4
CAP = 2
LANES = TARGETS * ROWS * RHS
SERVED = PANELS // 2
SLOTS = SERVED * CAP * RHS


def iota(shape, axis):
    return lax.broadcasted_iota(jnp.int32, shape, axis)


def ones_where(cond):
    return jnp.where(cond, 1.0, 0.0).astype(BF16)


def kernel(
    adj_hbm,
    near_hbm,
    pat_hbm,
    mask_hbm,
    spline_hbm,
    own_hbm,
    loc_hbm,
    inv_hbm,
    loads_ref,
    struct_ref,
    near_ref,
    spline_ref,
    inv_ref,
    own_ref,
    loc_ref,
    pat_ref,
    mask_ref,
    pool,
    mirror,
    relay,
    near_acc,
    mach_buf,
    place,
    pick,
    tab,
    ytab,
    ycomp,
    ztab,
    send_buf,
    recv_buf,
    load_sem,
    halo_send,
    halo_recv,
    relay_recv,
    pass_send,
    ring_send,
    ring_recv,
    mach_send,
    mach_recv,
    all_send,
    both_send,
    all_recv,
    core_send,
    core_recv,
    next_ready,
    wrap_ready,
    row_near,
    row_far,
    col_ready,
    mach_ready,
    mach_near,
    mach_far,
    row_in,
):
    m = lax.axis_index("mach")
    p = lax.axis_index("panel")
    z = p // RING
    y = p % RING
    core = m % 2
    parity = 1 - core
    barrier = pltpu.get_barrier_semaphore()

    def signal(sem, peer):
        pl.semaphore_signal(sem, inc=1, device_id=peer, device_id_type=MESH)

    def row_peer(j):
        return (m, z * RING + (y + j) % RING)

    def column_peer(j):
        return (m, ((z + j) % RING) * RING + y)

    def mach_peer(j):
        return ((m + j) % MACHS, p)

    half = RING // 2
    x = m // 2
    chips = MACHS // 2
    x_up = ((m + 2) % MACHS, p)
    x_down = ((m + MACHS - 2) % MACHS, p)
    other = (m + 1 - 2 * core, p)
    ends_row = (y == RING - 1) & (z < RING - 1)
    opens_row = (y == 0) & (z > 0)
    row_right = (m, z * RING + (y + 1) % RING)
    row_left = (m, z * RING + (y + RING - 1) % RING)

    @pl.when(x < chips - 1)
    def _():
        signal(barrier, x_up)

    @pl.when(x == 0)
    def _():
        signal(barrier, x_down)

    @pl.when(core == 1)
    def _():
        signal(barrier, other)

    @pl.when(y < half)
    def _():
        signal(barrier, row_right)

    @pl.when((y == 0) | (y > half))
    def _():
        signal(barrier, row_left)

    @pl.when(opens_row & (z != half))
    def _():
        signal(barrier, (m, p - 1))

    @pl.when(ends_row & (z == half - 1))
    def _():
        signal(barrier, (m, p + 1))

    def each(low, high, act):
        def step(k, carry):
            act(k)
            return carry

        lax.fori_loop(low, high, step, 0)

    each(z + 1, RING, lambda k: signal(barrier, (m, k * RING + y)))

    pairs = [
        (adj_hbm, pool.at[pl.ds(ROWS, ROWS)]),
        (own_hbm, own_ref),
        (loc_hbm, loc_ref),
        (pat_hbm, pat_ref),
        (mask_hbm, mask_ref),
        (near_hbm, near_ref),
        (spline_hbm, spline_ref),
        (inv_hbm, inv_ref),
    ]
    loads = [
        pltpu.make_async_copy(src, dst, load_sem.at[n]) for n, (src, dst) in enumerate(pairs)
    ]
    adj_load, own_load, loc_load, pat_load, mask_load, near_load, spline_load, inv_load = loads
    adj_load.start()

    def send(src, dst, send_sem, recv_sem, peer):
        copy = pltpu.make_async_remote_copy(
            src_ref=src,
            dst_ref=dst,
            send_sem=send_sem,
            recv_sem=recv_sem,
            device_id=peer,
            device_id_type=MESH,
        )
        copy.start()
        return copy

    def drain(ref, sem):
        pltpu.make_async_copy(ref, ref, sem).wait()

    row_count = jnp.where(y == 0, 0, jnp.where(y == half, 2, 1))
    later = (ends_row & (z != half - 1)) | (opens_row & (z == half))
    row_count = row_count + later.astype(jnp.int32)
    mach_count = jnp.where(x == 0, 0, jnp.where(x == chips - 1, 2, 1)) + 1 - core
    count = z + mach_count + row_count

    @pl.when(count > 0)
    def _():
        pl.semaphore_wait(barrier, count)

    adj = pool.at[pl.ds(ROWS, ROWS)]
    after_left = ((y > 0) & (y <= half)) | (opens_row & later)
    after_right = ((y >= half) & (y < RING - 1)) | (ends_row & later)
    before_left = (y > half) | (opens_row & jnp.logical_not(later))
    before_right = (y < half) | (ends_row & jnp.logical_not(later))

    @pl.when(z >= RING - 2)
    def _():
        signal(col_ready.at[z], (m, y))

    relayed = (z >= 2) & (z < RING - 2)

    @pl.when(relayed)
    def _():
        signal(col_ready.at[z], (m, p - 2 * RING))

    @pl.when(after_left)
    def _():
        signal(next_ready.at[1], (m, p - 1))

    @pl.when(after_right)
    def _():
        signal(next_ready.at[0], (m, p + 1))

    adj_load.wait()

    @pl.when(z >= half)
    def _():
        send(adj, mirror, halo_send.at[0], halo_recv.at[0], (m, p - half * RING))

    def to_left():
        send(adj, pool.at[pl.ds(2 * ROWS, ROWS)], halo_send.at[2], halo_recv.at[2], (m, p - 1))

    def to_right():
        send(adj, pool.at[pl.ds(0, ROWS)], halo_send.at[1], halo_recv.at[1], (m, p + 1))

    pl.when(after_left)(to_left)
    pl.when(after_right)(to_right)

    for copy in loads[1:]:
        copy.start()

    @pl.when(y == RING - 1)
    def _():
        signal(wrap_ready, row_right)

    @pl.when(core == 0)
    def _():
        signal(mach_ready, other)

    @pl.when(x > 0)
    def _():
        signal(mach_ready, x_down)

    @pl.when(x == chips - 1)
    def _():
        signal(mach_ready, x_up)

    def answer(k):
        told = (z >= RING - 2) & (k == 0) | relayed & (k == z - 2)

        @pl.when(jnp.logical_not(told))
        def _():
            signal(col_ready.at[z], (m, k * RING + y))

    each(0, z, answer)

    @pl.when((z >= 2) & (z < half))
    def _():
        send(adj, relay.at[z - 2], halo_send.at[0], relay_recv.at[z - 2], (m, p - z * RING))

    @pl.when(before_left)
    def _():
        pl.semaphore_wait(next_ready.at[0], 1)
        to_left()

    @pl.when(before_right)
    def _():
        pl.semaphore_wait(next_ready.at[1], 1)
        to_right()

    @pl.when(z < 2)
    def _():
        for k in range(2):

            @pl.when(z == k)
            def _():
                pl.semaphore_wait(col_ready.at[k + 2], 1)
                to = (m, p + 2 * RING)
                send(adj, relay.at[k], halo_send.at[0], relay_recv.at[k], to)

    @pl.when(y == 0)
    def _():
        pl.semaphore_wait(wrap_ready, 1)

    @pl.when(mach_count < 3)
    def _():
        pl.semaphore_wait(mach_ready, 3 - mach_count)

    signal(mach_near, x_up)
    signal(mach_near, x_down)
    signal(mach_near, other)
    signal(row_near, row_right)
    signal(row_near, row_left)

    own_load.wait()
    loc_load.wait()
    own = own_ref[...].astype(F32)
    loc = loc_ref[...].astype(F32)
    lane = iota((ROWS, LANES), 1)
    sub = iota((ROWS, LANES), 0)
    lane_s = lane // (ROWS * RHS)
    lane_i = (lane // RHS) % ROWS
    own_rows = jnp.zeros((ROWS, LANES), F32)
    loc_rows = jnp.zeros((ROWS, LANES), F32)
    for s in range(TARGETS):
        own_rows = jnp.where(lane_s == s, own[:, s : s + 1], own_rows)
        loc_rows = jnp.where(lane_s == s, loc[:, s : s + 1], loc_rows)
    mine = sub == lane_i
    own_lane = jnp.sum(jnp.where(mine, own_rows, 0.0), axis=0, keepdims=True)
    loc_lane = jnp.sum(jnp.where(mine, loc_rows, 0.0), axis=0, keepdims=True)
    same = jnp.zeros((ROWS, LANES), F32)
    for s in range(TARGETS):
        same = same + jnp.where(own[:, s : s + 1] == own_lane, 1.0, 0.0)
    slot = jnp.sum(jnp.where(sub < lane_i, same, 0.0), axis=0, keepdims=True)
    dest = own_lane * CAP + slot
    lane_r = (iota((1, LANES), 1) % RHS).astype(F32)
    chosen = ones_where(iota((PANELS * CAP, LANES), 0).astype(F32) == dest)
    weights = jnp.broadcast_to(
        jnp.where(lane_r == 0.0, loc_lane + 1.0, 0.0), (ROWS, LANES)
    ).astype(BF16)
    tab[...] = lax.dot_general(
        weights, chosen, (((1,), (1,)), ((), ())), preferred_element_type=F32
    )[:1]

    owner_row = iota((SLOTS, LANES), 0)
    owner_row = (owner_row // (CAP * RHS)) * (2 * CAP * RHS) + owner_row % (CAP * RHS)
    owner_row = owner_row + parity * (CAP * RHS)
    place[...] = ones_where(owner_row.astype(F32) == dest * RHS + lane_r)

    def pass_on(slot, child):
        pltpu.make_async_copy(relay.at[slot], relay.at[slot], relay_recv.at[slot]).wait()
        pl.semaphore_wait(col_ready.at[child], 1)
        send(
            relay.at[slot], mirror, pass_send.at[slot], halo_recv.at[0], (m, child * RING + y)
        )

    @pl.when(z == 2)
    def _():
        pass_on(0, half)

    @pl.when(z == 3)
    def _():
        pass_on(1, half + 1)

    @pl.when(z == 0)
    def _():
        pass_on(0, RING - 2)
        pass_on(1, RING - 1)

    pl.semaphore_wait(mach_near, 3)
    signal(mach_far, other)
    pl.semaphore_wait(row_near, 2)
    for j in (1, 2, RING - 2, RING - 1):
        signal(row_far, row_peer(j))

    pat_load.wait()
    near_load.wait()

    @pl.when(p > 0)
    def _():
        drain(mirror, halo_recv.at[1])

    @pl.when(p < PANELS - 1)
    def _():
        drain(mirror, halo_recv.at[2])

    for i in range(ROWS):
        picked = [
            pool[jnp.clip(pat_ref[i, k] - p * ROWS + ROWS, 0, 3 * ROWS - 1)]
            for k in range(2, NNZ)
        ]
        near_acc[RHS * i : RHS * (i + 1), :] = jnp.dot(
            pool[ROWS + i], near_ref[i, 0], preferred_element_type=F32
        ) + jnp.dot(
            jnp.concatenate(picked, axis=1),
            near_ref[i, 2:NNZ].reshape((NNZ - 2) * 128, 128),
            preferred_element_type=F32,
        )

    mask_load.wait()
    row32 = iota((ROWS * RHS, 1), 0)
    gate = jnp.zeros((ROWS * RHS, 1), F32)
    for r in range(RHS):
        gate = jnp.where(row32 % RHS == r, mask_ref[0, r].astype(F32), gate)

    pl.semaphore_wait(row_far, 4)
    for j in range(1, RING):
        send(tab, ytab.at[y], ring_send.at[0], ring_recv.at[0], row_peer(j))
    ytab[y] = tab[...]

    for k in range(1, RING):
        early = (k == z + 2) & (z < half) | (z == 0) & (k >= RING - 2)

        @pl.when((k > z) & jnp.logical_not(early))
        def _():
            pl.semaphore_wait(col_ready.at[k], 1)

    for j in range(1, RING):
        signal(row_in, column_peer(j))

    pl.semaphore_wait(mach_far, 1)
    drain(mirror, halo_recv.at[0])
    for i in range(ROWS):
        near_acc[RHS * i : RHS * (i + 1), :] += jnp.dot(
            mirror[i], near_ref[i, 1], preferred_element_type=F32
        )
    masked = near_acc[...] * gate
    mach_buf[m] = masked.astype(BF16)
    for j in (4, 3, 5, 2, 6, 1, 7):
        send(mach_buf.at[m], mach_buf.at[m], mach_send, mach_recv, mach_peer(j))
    loads_ref[...] = masked

    spline_load.wait()
    drain(mach_buf.at[pl.ds(0, MACHS - 1)], mach_recv)
    total = mach_buf[0].astype(F32)
    for j in range(1, MACHS):
        total = total + mach_buf[j].astype(F32)
    high = total.astype(BF16).astype(F32)
    both = jnp.concatenate([high, total - high], axis=0)
    row64 = (iota((2 * ROWS * RHS, 128), 0) // RHS) % ROWS
    spread = jnp.concatenate(
        [jnp.where(row64 == i, both, 0.0).astype(BF16) for i in range(ROWS)], axis=1
    )
    contrib = []
    for s in range(TARGETS):
        out = jnp.dot(
            spread,
            spline_ref[:, s].reshape(ROWS * 128, 128),
            preferred_element_type=F32,
        )
        contrib.append((out[: ROWS * RHS] + out[ROWS * RHS :]).astype(BF16))
    packed = jnp.dot(
        place[...], jnp.concatenate(contrib, axis=0), preferred_element_type=F32
    )
    send_buf[...] = packed.astype(BF16).reshape(SERVED, CAP * RHS, 128)

    serves = y % 2 == parity
    first = p < 2
    pl.semaphore_wait(row_in, RING - 1)

    def post(j, carry):
        far = j // (RING // 2)
        side = 1 - 2 * (far % 2)
        to_z = (z + RING // 2 + side * ((far + 1) // 2) + RING) % RING
        to_y = ((y // 2 + 2 + j % (RING // 2)) % (RING // 2)) * 2 + parity
        peer = to_z * RING + to_y

        @pl.when((peer != p) & (peer != parity))
        def _():
            send(send_buf.at[peer // 2], recv_buf.at[p], all_send, all_recv, (m, peer))

        return carry

    send(send_buf.at[0], recv_buf.at[p], both_send, all_recv, (m + 1 - 2 * core, parity))

    @pl.when(p != parity)
    def _():
        send(send_buf.at[0], recv_buf.at[p], all_send, all_recv, (m, parity))

    lax.fori_loop(0, SERVED // 2, post, 0)
    drain(ytab.at[pl.ds(0, RING - 1)], ring_recv.at[0])
    sub8 = iota((RING, 128), 0)
    comp = jnp.zeros((RING, 128), F32)
    for j in range(RING):
        comp = jnp.where(sub8 == j, ytab[j], comp)
    ycomp[...] = comp.astype(BF16)
    for j in range(1, RING):
        send(ycomp, ztab.at[z], ring_send.at[1], ring_recv.at[1], column_peer(j))
    ztab[z] = ycomp[...]
    lax.fori_loop(SERVED // 2, SERVED, post, 0)

    drain(ztab.at[pl.ds(0, RING - 1)], ring_recv.at[1])
    inv_load.wait()

    @pl.when(serves)
    def _():
        recv_buf[p] = send_buf[p // 2]

    @pl.when(serves | first)
    def _():
        lane5 = iota((128, PANELS * CAP * RHS), 1)
        wanted = ones_where(iota((128, PANELS * CAP * RHS), 0) == p * CAP + (lane5 // RHS) % CAP)
        blocks = jnp.dot(
            ztab[...].astype(F32).reshape(PANELS, 128).astype(BF16), wanted, preferred_element_type=F32
        )
        shape = (PANELS, PANELS * CAP * RHS)
        from_panel = iota(shape, 0) == iota(shape, 1) // (CAP * RHS)
        block_lane = jnp.sum(jnp.where(from_panel, blocks, 0.0), axis=0, keepdims=True)
        shape = (ROWS * RHS, PANELS * CAP * RHS)
        row5 = iota(shape, 0)
        col5 = iota(shape, 1)
        pick[...] = ones_where(
            (block_lane == (row5 // RHS + 1).astype(F32)) & (col5 % RHS == row5 % RHS)
        )

        @pl.when(serves)
        def _():
            drain(recv_buf.at[pl.ds(0, PANELS - 1)], all_recv)

        @pl.when(jnp.logical_not(serves))
        def _():
            drain(recv_buf, all_recv)

        found = jnp.dot(
            pick[...],
            recv_buf[...].reshape(PANELS * CAP * RHS, 128),
            preferred_element_type=F32,
        )
        row_block = iota((ROWS * RHS, 128), 0) // RHS
        wide = jnp.concatenate(
            [jnp.where(row_block == t, found, 0.0).astype(BF16) for t in range(ROWS)], axis=1
        )
        struct_ref[...] = jnp.dot(
            wide, inv_ref[...].reshape(ROWS * 128, 128), preferred_element_type=F32
        )

    alone = jnp.logical_not(first)

    @pl.when(serves & alone)
    def _():
        send(struct_ref, struct_ref, core_send, core_recv, other)
        drain(struct_ref, core_send)

    @pl.when(jnp.logical_not(serves) & alone)
    def _():
        drain(struct_ref, core_recv)

    @pl.when(serves)
    def _():
        drain(send_buf.at[pl.ds(0, SERVED - 1)], all_send)

    @pl.when(jnp.logical_not(serves))
    def _():
        drain(send_buf, all_send)

    drain(send_buf.at[pl.ds(0, 1)], both_send)

    drain(mirror, halo_send.at[0])

    @pl.when(p < PANELS - 1)
    def _():
        drain(mirror, halo_send.at[1])

    @pl.when(p > 0)
    def _():
        drain(mirror, halo_send.at[2])

    @pl.when((z == 0) | (z == 2))
    def _():
        drain(mirror, pass_send.at[0])

    @pl.when((z == 0) | (z == 3))
    def _():
        drain(mirror, pass_send.at[1])

    for stage, ref in enumerate((ytab, ztab)):
        drain(ref.at[pl.ds(0, RING - 1)], ring_send.at[stage])
    drain(mach_buf.at[pl.ds(0, MACHS - 1)], mach_send)


def hand_on(loads_ref, struct_ref, loads_out, struct_out):
    loads_out[...] = loads_ref[...]
    struct_out[...] = struct_ref[...]


def on_device(adjoint, near, pattern, mask, spline, owner, local, inverse):
    vmem = pl.BlockSpec(memory_space=pltpu.VMEM)
    hbm = pl.BlockSpec(memory_space=pl.ANY)
    rows = ROWS * RHS
    dma = pltpu.SemaphoreType.DMA
    regular = pltpu.SemaphoreType.REGULAR
    loads, struct = pl.pallas_call(
        kernel,
        out_shape=(
            pltpu.VMEM((rows, 128), F32),
            pltpu.VMEM((rows, 128), F32),
        ),
        in_specs=[hbm] * 8,
        out_specs=(vmem, vmem),
        scratch_shapes=[
            pltpu.VMEM((ROWS, NNZ, 128, 128), BF16),
            pltpu.VMEM((ROWS, TARGETS, 128, 128), BF16),
            pltpu.VMEM((ROWS, 128, 128), BF16),
            pltpu.VMEM((ROWS, TARGETS), jnp.int32),
            pltpu.VMEM((ROWS, TARGETS), jnp.int32),
            pltpu.SMEM((ROWS, NNZ), jnp.int32),
            pltpu.SMEM((1, RHS), jnp.int32),
            pltpu.VMEM((3 * ROWS, RHS, 128), BF16),
            pltpu.VMEM((ROWS, RHS, 128), BF16),
            pltpu.VMEM((2, ROWS, RHS, 128), BF16),
            pltpu.VMEM((rows, 128), F32),
            pltpu.VMEM((MACHS, rows, 128), BF16),
            pltpu.VMEM((SLOTS, LANES), BF16),
            pltpu.VMEM((rows, PANELS * CAP * RHS), BF16),
            pltpu.VMEM((1, 128), F32),
            pltpu.VMEM((RING, 1, 128), F32),
            pltpu.VMEM((RING, 128), BF16),
            pltpu.VMEM((RING, RING, 128), BF16),
            pltpu.VMEM((SERVED, CAP * RHS, 128), BF16),
            pltpu.VMEM((PANELS, CAP * RHS, 128), BF16),
            dma((8,)),
            dma((3,)),
            dma((3,)),
            dma((2,)),
            dma((2,)),
            dma((2,)),
            dma((2,)),
            dma,
            dma,
            dma,
            dma,
            dma,
            dma,
            dma,
            regular((2,)),
            regular,
            regular,
            regular,
            regular((RING,)),
            regular,
            regular,
            regular,
            regular,
        ],
        compiler_params=pltpu.CompilerParams(collective_id=0, has_side_effects=True),
        name="load_transfer",
    )(adjoint[0], near[0], pattern, mask, spline, owner, local, inverse)
    out = jax.ShapeDtypeStruct((rows, 128), F32)
    loads, struct = pl.pallas_call(
        hand_on,
        out_shape=(out, out),
        in_specs=[vmem, vmem],
        out_specs=(vmem, vmem),
        name="hand_on",
        compiler_params=pltpu.CompilerParams(vmem_limit_bytes=1 << 20),
    )(loads, struct)
    return loads.reshape(1, ROWS, RHS, 128), struct.reshape(ROWS, RHS, 128)


def solution(mesh):
    in_specs = (
        P("mach", "panel", None, None),
        P("mach", "panel", None, None, None),
        P("panel", None),
        P("mach", None),
        P("panel", None, None, None),
        P("panel", None),
        P("panel", None),
        P("panel", None, None),
    )
    out_specs = (P("mach", "panel", None, None), P("panel", None, None))
    return jax.shard_map(
        on_device, mesh=mesh, in_specs=in_specs, out_specs=out_specs, check_vma=False
    )
```

```python
import jax
import jax.numpy as jnp
from jax import lax
from jax.experimental import pallas as pl
from jax.experimental.pallas import tpu as pltpu
from jax.sharding import PartitionSpec as P

MESH = pl.DeviceIdType.MESH
F32 = jnp.float32
BF16 = jnp.bfloat16
MACHS = 8
PANELS = 64
RING = 8
ROWS = 8
NNZ = 8
TARGETS = 6
RHS = 4
CAP = 2
LANES = TARGETS * ROWS * RHS
SERVED = PANELS // 2
SLOTS = SERVED * CAP * RHS


def iota(shape, axis):
    return lax.broadcasted_iota(jnp.int32, shape, axis)


def ones_where(cond):
    return jnp.where(cond, 1.0, 0.0).astype(BF16)


def kernel(
    adj_hbm,
    near_hbm,
    pat_hbm,
    mask_hbm,
    spline_hbm,
    own_hbm,
    loc_hbm,
    inv_hbm,
    loads_ref,
    struct_ref,
    near_ref,
    spline_ref,
    inv_ref,
    own_ref,
    loc_ref,
    pat_ref,
    mask_ref,
    pool,
    mirror,
    relay,
    near_acc,
    mach_buf,
    place,
    pick,
    tab,
    ytab,
    ycomp,
    ztab,
    send_buf,
    recv_buf,
    load_sem,
    halo_send,
    halo_recv,
    relay_recv,
    pass_send,
    ring_send,
    ring_recv,
    mach_send,
    mach_recv,
    all_send,
    all_recv,
    core_send,
    core_recv,
    next_ready,
    wrap_ready,
    row_near,
    row_far,
    col_ready,
    mach_ready,
    mach_near,
    mach_far,
    row_in,
):
    m = lax.axis_index("mach")
    p = lax.axis_index("panel")
    z = p // RING
    y = p % RING
    core = m % 2
    parity = 1 - core
    barrier = pltpu.get_barrier_semaphore()

    def signal(sem, peer):
        pl.semaphore_signal(sem, inc=1, device_id=peer, device_id_type=MESH)

    def row_peer(j):
        return (m, z * RING + (y + j) % RING)

    def column_peer(j):
        return (m, ((z + j) % RING) * RING + y)

    def mach_peer(j):
        return ((m + j) % MACHS, p)

    half = RING // 2
    x = m // 2
    chips = MACHS // 2
    x_up = ((m + 2) % MACHS, p)
    x_down = ((m + MACHS - 2) % MACHS, p)
    other = (m + 1 - 2 * core, p)
    ends_row = (y == RING - 1) & (z < RING - 1)
    opens_row = (y == 0) & (z > 0)
    row_right = (m, z * RING + (y + 1) % RING)
    row_left = (m, z * RING + (y + RING - 1) % RING)

    @pl.when(x < chips - 1)
    def _():
        signal(barrier, x_up)

    @pl.when(x == 0)
    def _():
        signal(barrier, x_down)

    @pl.when(core == 1)
    def _():
        signal(barrier, other)

    @pl.when(y < half)
    def _():
        signal(barrier, row_right)

    @pl.when((y == 0) | (y > half))
    def _():
        signal(barrier, row_left)

    @pl.when(opens_row & (z != half))
    def _():
        signal(barrier, (m, p - 1))

    @pl.when(ends_row & (z == half - 1))
    def _():
        signal(barrier, (m, p + 1))

    def each(low, high, act):
        def step(k, carry):
            act(k)
            return carry

        lax.fori_loop(low, high, step, 0)

    each(z + 1, RING, lambda k: signal(barrier, (m, k * RING + y)))

    pairs = [
        (adj_hbm, pool.at[pl.ds(ROWS, ROWS)]),
        (own_hbm, own_ref),
        (loc_hbm, loc_ref),
        (pat_hbm, pat_ref),
        (mask_hbm, mask_ref),
        (near_hbm, near_ref),
        (spline_hbm, spline_ref),
        (inv_hbm, inv_ref),
    ]
    loads = [
        pltpu.make_async_copy(src, dst, load_sem.at[n]) for n, (src, dst) in enumerate(pairs)
    ]
    adj_load, own_load, loc_load, pat_load, mask_load, near_load, spline_load, inv_load = loads
    adj_load.start()

    def send(src, dst, send_sem, recv_sem, peer):
        copy = pltpu.make_async_remote_copy(
            src_ref=src,
            dst_ref=dst,
            send_sem=send_sem,
            recv_sem=recv_sem,
            device_id=peer,
            device_id_type=MESH,
        )
        copy.start()
        return copy

    def drain(ref, sem):
        pltpu.make_async_copy(ref, ref, sem).wait()

    row_count = jnp.where(y == 0, 0, jnp.where(y == half, 2, 1))
    later = (ends_row & (z != half - 1)) | (opens_row & (z == half))
    row_count = row_count + later.astype(jnp.int32)
    mach_count = jnp.where(x == 0, 0, jnp.where(x == chips - 1, 2, 1)) + 1 - core
    count = z + mach_count + row_count

    @pl.when(count > 0)
    def _():
        pl.semaphore_wait(barrier, count)

    adj = pool.at[pl.ds(ROWS, ROWS)]
    after_left = ((y > 0) & (y <= half)) | (opens_row & later)
    after_right = ((y >= half) & (y < RING - 1)) | (ends_row & later)
    before_left = (y > half) | (opens_row & jnp.logical_not(later))
    before_right = (y < half) | (ends_row & jnp.logical_not(later))

    @pl.when(z >= RING - 2)
    def _():
        signal(col_ready.at[z - (RING - 3)], (m, y))

    relayed = (z >= 2) & (z < RING - 2)

    @pl.when(relayed)
    def _():
        signal(col_ready.at[0], (m, p - 2 * RING))

    @pl.when(after_left)
    def _():
        signal(next_ready.at[1], (m, p - 1))

    @pl.when(after_right)
    def _():
        signal(next_ready.at[0], (m, p + 1))

    adj_load.wait()

    @pl.when(z >= half)
    def _():
        send(adj, mirror, halo_send.at[0], halo_recv.at[0], (m, p - half * RING))

    def to_left():
        send(adj, pool.at[pl.ds(2 * ROWS, ROWS)], halo_send.at[2], halo_recv.at[2], (m, p - 1))

    def to_right():
        send(adj, pool.at[pl.ds(0, ROWS)], halo_send.at[1], halo_recv.at[1], (m, p + 1))

    pl.when(after_left)(to_left)
    pl.when(after_right)(to_right)

    for copy in loads[1:]:
        copy.start()

    @pl.when(y == RING - 1)
    def _():
        signal(wrap_ready, row_right)

    @pl.when(core == 0)
    def _():
        signal(mach_ready, other)

    @pl.when(x > 0)
    def _():
        signal(mach_ready, x_down)

    @pl.when(x == chips - 1)
    def _():
        signal(mach_ready, x_up)

    def answer(k):
        told = (z >= RING - 2) & (k == 0) | relayed & (k == z - 2)

        @pl.when(jnp.logical_not(told))
        def _():
            signal(col_ready.at[3], (m, k * RING + y))

    each(0, z, answer)

    @pl.when((z >= 2) & (z < half))
    def _():
        send(adj, relay.at[z - 2], halo_send.at[0], relay_recv.at[z - 2], (m, p - z * RING))

    @pl.when(before_left)
    def _():
        pl.semaphore_wait(next_ready.at[0], 1)
        to_left()

    @pl.when(before_right)
    def _():
        pl.semaphore_wait(next_ready.at[1], 1)
        to_right()

    @pl.when(z < 2)
    def _():
        for k in range(2):

            @pl.when(z == k)
            def _():
                pl.semaphore_wait(col_ready.at[0], 1)
                to = (m, p + 2 * RING)
                send(adj, relay.at[k], halo_send.at[0], relay_recv.at[k], to)

    @pl.when(y == 0)
    def _():
        pl.semaphore_wait(wrap_ready, 1)

    @pl.when(mach_count < 3)
    def _():
        pl.semaphore_wait(mach_ready, 3 - mach_count)

    signal(mach_near, x_up)
    signal(mach_near, x_down)
    signal(mach_near, other)
    signal(row_near, row_right)
    signal(row_near, row_left)

    own_load.wait()
    loc_load.wait()
    own = own_ref[...].astype(F32)
    loc = loc_ref[...].astype(F32)
    lane = iota((ROWS, LANES), 1)
    sub = iota((ROWS, LANES), 0)
    lane_s = lane // (ROWS * RHS)
    lane_i = (lane // RHS) % ROWS
    own_rows = jnp.zeros((ROWS, LANES), F32)
    loc_rows = jnp.zeros((ROWS, LANES), F32)
    for s in range(TARGETS):
        own_rows = jnp.where(lane_s == s, own[:, s : s + 1], own_rows)
        loc_rows = jnp.where(lane_s == s, loc[:, s : s + 1], loc_rows)
    mine = sub == lane_i
    own_lane = jnp.sum(jnp.where(mine, own_rows, 0.0), axis=0, keepdims=True)
    loc_lane = jnp.sum(jnp.where(mine, loc_rows, 0.0), axis=0, keepdims=True)
    same = jnp.zeros((ROWS, LANES), F32)
    for s in range(TARGETS):
        same = same + jnp.where(own[:, s : s + 1] == own_lane, 1.0, 0.0)
    slot = jnp.sum(jnp.where(sub < lane_i, same, 0.0), axis=0, keepdims=True)
    dest = own_lane * CAP + slot
    lane_r = (iota((1, LANES), 1) % RHS).astype(F32)
    chosen = ones_where(iota((PANELS * CAP, LANES), 0).astype(F32) == dest)
    weights = jnp.broadcast_to(
        jnp.where(lane_r == 0.0, loc_lane + 1.0, 0.0), (ROWS, LANES)
    ).astype(BF16)
    tab[...] = lax.dot_general(
        weights, chosen, (((1,), (1,)), ((), ())), preferred_element_type=F32
    )[:1]

    owner_row = iota((SLOTS, LANES), 0)
    owner_row = (owner_row // (CAP * RHS)) * (2 * CAP * RHS) + owner_row % (CAP * RHS)
    owner_row = owner_row + parity * (CAP * RHS)
    place[...] = ones_where(owner_row.astype(F32) == dest * RHS + lane_r)

    def pass_on(slot, child, ready):
        pltpu.make_async_copy(relay.at[slot], relay.at[slot], relay_recv.at[slot]).wait()
        pl.semaphore_wait(col_ready.at[ready], 1)
        send(
            relay.at[slot], mirror, pass_send.at[slot], halo_recv.at[0], (m, child * RING + y)
        )

    @pl.when(z == 2)
    def _():
        pass_on(0, half, 0)

    @pl.when(z == 3)
    def _():
        pass_on(1, half + 1, 0)

    @pl.when(z == 0)
    def _():
        pass_on(0, RING - 2, 1)
        pass_on(1, RING - 1, 2)

    pl.semaphore_wait(mach_near, 3)
    signal(mach_far, other)
    pl.semaphore_wait(row_near, 2)
    for j in (1, 2, RING - 2, RING - 1):
        signal(row_far, row_peer(j))

    pat_load.wait()
    near_load.wait()

    @pl.when(p > 0)
    def _():
        drain(mirror, halo_recv.at[1])

    @pl.when(p < PANELS - 1)
    def _():
        drain(mirror, halo_recv.at[2])

    for i in range(ROWS):
        picked = [
            pool[jnp.clip(pat_ref[i, k] - p * ROWS + ROWS, 0, 3 * ROWS - 1)]
            for k in range(2, NNZ)
        ]
        near_acc[RHS * i : RHS * (i + 1), :] = jnp.dot(
            pool[ROWS + i], near_ref[i, 0], preferred_element_type=F32
        ) + jnp.dot(
            jnp.concatenate(picked, axis=1),
            near_ref[i, 2:NNZ].reshape((NNZ - 2) * 128, 128),
            preferred_element_type=F32,
        )

    mask_load.wait()
    row32 = iota((ROWS * RHS, 1), 0)
    gate = jnp.zeros((ROWS * RHS, 1), F32)
    for r in range(RHS):
        gate = jnp.where(row32 % RHS == r, mask_ref[0, r].astype(F32), gate)

    pl.semaphore_wait(row_far, 4)
    for j in range(1, RING):
        send(tab, ytab.at[y], ring_send.at[0], ring_recv.at[0], row_peer(j))
    ytab[y] = tab[...]

    others = RING - 1 - z - (z < half).astype(jnp.int32) - jnp.where(z == 0, 2, 0)

    @pl.when(others > 0)
    def _():
        pl.semaphore_wait(col_ready.at[3], others)

    for j in range(1, RING):
        signal(row_in, column_peer(j))

    pl.semaphore_wait(mach_far, 1)
    drain(mirror, halo_recv.at[0])
    for i in range(ROWS):
        near_acc[RHS * i : RHS * (i + 1), :] += jnp.dot(
            mirror[i], near_ref[i, 1], preferred_element_type=F32
        )
    masked = near_acc[...] * gate
    mach_buf[m] = masked.astype(BF16)
    for j in (4, 3, 5, 2, 6, 1, 7):
        send(mach_buf.at[m], mach_buf.at[m], mach_send, mach_recv, mach_peer(j))
    loads_ref[...] = masked

    spline_load.wait()
    drain(mach_buf.at[pl.ds(0, MACHS - 1)], mach_recv)
    total = mach_buf[0].astype(F32)
    for j in range(1, MACHS):
        total = total + mach_buf[j].astype(F32)
    high = total.astype(BF16).astype(F32)
    both = jnp.concatenate([high, total - high], axis=0)
    row64 = (iota((2 * ROWS * RHS, 128), 0) // RHS) % ROWS
    spread = jnp.concatenate(
        [jnp.where(row64 == i, both, 0.0).astype(BF16) for i in range(ROWS)], axis=1
    )
    contrib = []
    for s in range(TARGETS):
        out = jnp.dot(
            spread,
            spline_ref[:, s].reshape(ROWS * 128, 128),
            preferred_element_type=F32,
        )
        contrib.append((out[: ROWS * RHS] + out[ROWS * RHS :]).astype(BF16))
    rows = jnp.concatenate(contrib, axis=0)

    def pack(low, high):
        width = CAP * RHS
        packed = jnp.dot(place[low * width : high * width], rows, preferred_element_type=F32)
        send_buf[low:high] = packed.astype(BF16).reshape(high - low, width, 128)

    pack(0, 2)

    serves = y % 2 == parity
    first = p < 2
    pl.semaphore_wait(row_in, RING - 1)

    def post(j, carry):
        far = j // (RING // 2)
        side = 1 - 2 * (far % 2)
        to_z = (z + RING // 2 + side * ((far + 1) // 2) + RING) % RING
        to_y = ((y // 2 + 2 + j % (RING // 2)) % (RING // 2)) * 2 + parity
        peer = to_z * RING + to_y

        @pl.when((peer != p) & (peer != parity))
        def _():
            send(send_buf.at[peer // 2], recv_buf.at[p], all_send, all_recv, (m, peer))

        return carry

    send(send_buf.at[0], recv_buf.at[p], all_send, all_recv, (m + 1 - 2 * core, parity))

    @pl.when(p != parity)
    def _():
        send(send_buf.at[0], recv_buf.at[p], all_send, all_recv, (m, parity))

    pack(2, SERVED)
    lax.fori_loop(0, SERVED // 2, post, 0)
    drain(ytab.at[pl.ds(0, RING - 1)], ring_recv.at[0])
    sub8 = iota((RING, 128), 0)
    comp = jnp.zeros((RING, 128), F32)
    for j in range(RING):
        comp = jnp.where(sub8 == j, ytab[j], comp)
    ycomp[...] = comp.astype(BF16)
    for j in range(1, RING):
        send(ycomp, ztab.at[z], ring_send.at[1], ring_recv.at[1], column_peer(j))
    ztab[z] = ycomp[...]
    lax.fori_loop(SERVED // 2, SERVED, post, 0)

    drain(ztab.at[pl.ds(0, RING - 1)], ring_recv.at[1])
    inv_load.wait()

    @pl.when(serves)
    def _():
        recv_buf[p] = send_buf[p // 2]

    @pl.when(serves | first)
    def _():
        lane5 = iota((128, PANELS * CAP * RHS), 1)
        wanted = ones_where(iota((128, PANELS * CAP * RHS), 0) == p * CAP + (lane5 // RHS) % CAP)
        blocks = jnp.dot(
            ztab[...].astype(F32).reshape(PANELS, 128).astype(BF16), wanted, preferred_element_type=F32
        )
        shape = (PANELS, PANELS * CAP * RHS)
        from_panel = iota(shape, 0) == iota(shape, 1) // (CAP * RHS)
        block_lane = jnp.sum(jnp.where(from_panel, blocks, 0.0), axis=0, keepdims=True)
        shape = (ROWS * RHS, PANELS * CAP * RHS)
        row5 = iota(shape, 0)
        col5 = iota(shape, 1)
        pick[...] = ones_where(
            (block_lane == (row5 // RHS + 1).astype(F32)) & (col5 % RHS == row5 % RHS)
        )

        @pl.when(serves)
        def _():
            drain(recv_buf.at[pl.ds(0, PANELS - 1)], all_recv)

        @pl.when(jnp.logical_not(serves))
        def _():
            drain(recv_buf, all_recv)

        found = jnp.dot(
            pick[...],
            recv_buf[...].reshape(PANELS * CAP * RHS, 128),
            preferred_element_type=F32,
        )
        row_block = iota((ROWS * RHS, 128), 0) // RHS
        wide = jnp.concatenate(
            [jnp.where(row_block == t, found, 0.0).astype(BF16) for t in range(ROWS)], axis=1
        )
        struct_ref[...] = jnp.dot(
            wide, inv_ref[...].reshape(ROWS * 128, 128), preferred_element_type=F32
        )

    alone = jnp.logical_not(first)

    @pl.when(serves & alone)
    def _():
        send(struct_ref, struct_ref, core_send, core_recv, other)
        drain(struct_ref, core_send)

    @pl.when(jnp.logical_not(serves) & alone)
    def _():
        drain(struct_ref, core_recv)

    @pl.when(serves)
    def _():
        drain(send_buf, all_send)

    @pl.when(jnp.logical_not(serves))
    def _():
        drain(recv_buf.at[pl.ds(0, SERVED + 1)], all_send)


    drain(mirror, halo_send.at[0])

    @pl.when(p < PANELS - 1)
    def _():
        drain(mirror, halo_send.at[1])

    @pl.when(p > 0)
    def _():
        drain(mirror, halo_send.at[2])

    @pl.when((z == 0) | (z == 2))
    def _():
        drain(mirror, pass_send.at[0])

    @pl.when((z == 0) | (z == 3))
    def _():
        drain(mirror, pass_send.at[1])

    for stage, ref in enumerate((ytab, ztab)):
        drain(ref.at[pl.ds(0, RING - 1)], ring_send.at[stage])
    drain(mach_buf.at[pl.ds(0, MACHS - 1)], mach_send)


def hand_on(loads_ref, struct_ref, loads_out, struct_out):
    loads_out[...] = loads_ref[...]
    struct_out[...] = struct_ref[...]


def on_device(adjoint, near, pattern, mask, spline, owner, local, inverse):
    vmem = pl.BlockSpec(memory_space=pltpu.VMEM)
    hbm = pl.BlockSpec(memory_space=pl.ANY)
    rows = ROWS * RHS
    dma = pltpu.SemaphoreType.DMA
    regular = pltpu.SemaphoreType.REGULAR
    loads, struct = pl.pallas_call(
        kernel,
        out_shape=(
            pltpu.VMEM((rows, 128), F32),
            pltpu.VMEM((rows, 128), F32),
        ),
        in_specs=[hbm] * 8,
        out_specs=(vmem, vmem),
        scratch_shapes=[
            pltpu.VMEM((ROWS, NNZ, 128, 128), BF16),
            pltpu.VMEM((ROWS, TARGETS, 128, 128), BF16),
            pltpu.VMEM((ROWS, 128, 128), BF16),
            pltpu.VMEM((ROWS, TARGETS), jnp.int32),
            pltpu.VMEM((ROWS, TARGETS), jnp.int32),
            pltpu.SMEM((ROWS, NNZ), jnp.int32),
            pltpu.SMEM((1, RHS), jnp.int32),
            pltpu.VMEM((3 * ROWS, RHS, 128), BF16),
            pltpu.VMEM((ROWS, RHS, 128), BF16),
            pltpu.VMEM((2, ROWS, RHS, 128), BF16),
            pltpu.VMEM((rows, 128), F32),
            pltpu.VMEM((MACHS, rows, 128), BF16),
            pltpu.VMEM((SLOTS, LANES), BF16),
            pltpu.VMEM((rows, PANELS * CAP * RHS), BF16),
            pltpu.VMEM((1, 128), F32),
            pltpu.VMEM((RING, 1, 128), F32),
            pltpu.VMEM((RING, 128), BF16),
            pltpu.VMEM((RING, RING, 128), BF16),
            pltpu.VMEM((SERVED, CAP * RHS, 128), BF16),
            pltpu.VMEM((PANELS, CAP * RHS, 128), BF16),
            dma((8,)),
            dma((3,)),
            dma((3,)),
            dma((2,)),
            dma((2,)),
            dma((2,)),
            dma((2,)),
            dma,
            dma,
            dma,
            dma,
            dma,
            dma,
            regular((2,)),
            regular,
            regular,
            regular,
            regular((4,)),
            regular,
            regular,
            regular,
            regular,
        ],
        compiler_params=pltpu.CompilerParams(collective_id=0, has_side_effects=True),
        name="load_transfer",
    )(adjoint[0], near[0], pattern, mask, spline, owner, local, inverse)
    out = jax.ShapeDtypeStruct((rows, 128), F32)
    loads, struct = pl.pallas_call(
        hand_on,
        out_shape=(out, out),
        in_specs=[vmem, vmem],
        out_specs=(vmem, vmem),
        name="hand_on",
        compiler_params=pltpu.CompilerParams(vmem_limit_bytes=1 << 20),
    )(loads, struct)
    return loads.reshape(1, ROWS, RHS, 128), struct.reshape(ROWS, RHS, 128)


def solution(mesh):
    in_specs = (
        P("mach", "panel", None, None),
        P("mach", "panel", None, None, None),
        P("panel", None),
        P("mach", None),
        P("panel", None, None, None),
        P("panel", None),
        P("panel", None),
        P("panel", None, None),
    )
    out_specs = (P("mach", "panel", None, None), P("panel", None, None))
    return jax.shard_map(
        on_device, mesh=mesh, in_specs=in_specs, out_specs=out_specs, check_vma=False
    )
```
